256 devices in a mesh: group: 4 (over y), rank: 64 (over z, x, core).
Axes of the slice: x: 4, y: 4, z: 8, core: 2. Of those that a mesh axis runs over, the one named last changes fastest.
Arguments:
- queries: bfloat16 [65536, 2048], P(('group', 'rank')), may hold values from -32 to 32
- key_rows: bfloat16 [65536, 2048], P(('group', 'rank')), may hold values from -6 to 6
- value_rows: bfloat16 [65536, 2048], P(('group', 'rank')), may hold values from -6 to 6
- tile_links: int32 [512, 8], P(('group', 'rank')), may hold values from 0 to 15, as said below
- link_counts: int32 [512], P(('group', 'rank')), may hold values from 1 to 8, 2048 in all
Outputs:
- attended: bfloat16 [65536, 2048], P(('group', 'rank'))
The draws below stay inside these ranges and needn't reach their ends.
Inputs may be any that keep to these rules, and one draw needn't show every extreme that they name: `tile_links`: each row names 8 different candidates.
All inputs are finite; a program needn't handle non-finite values. No bound on the sum of `link_counts` on one device may be relied on, other than what follows from the above.
Results may differ from the reference program's by a relative error of at most 0.0045.
Values may be sent and summed in bfloat16 or wider, within the bound.
No kernel may reach another device: no remote copies, remote signals or barrier semaphores. Data moves between devices by JAX's collectives and lax.ppermute only.
A program may use at most 128 MiB of HBM per device.

```python
import math
import jax
import jax.numpy as jnp
import numpy as np
from jax import lax

H = 16
HD = 128
TILE = 128
TPD = 2
LMAX = 8
W = 2048
GROUPS = 4
RANKS = 64
NTILES = 512
NODES = 65536
CAND = 16


def shared_rows(key):
    base = jax.random.fold_in(key, 7)
    query_key, key_key = jax.random.split(base, 2)
    query_draw = jnp.clip(jax.random.normal(query_key, (NODES, W), jnp.float32), -6.0, 6.0)
    key_draw = jnp.clip(jax.random.normal(key_key, (NODES, W), jnp.float32), -6.0, 6.0)
    return (query_draw, key_draw)


def draw_queries(key, part):
    return shared_rows(key)[0].astype(jnp.bfloat16)


def draw_key_rows(key, part):
    return shared_rows(key)[1].astype(jnp.bfloat16)


def draw_tile_links(key, part):
    link_key = jax.random.fold_in(key, 11)
    scores = jax.random.randint(link_key, (NTILES, CAND), 0, 2 ** 20) * CAND + jnp.arange(CAND, dtype=jnp.int32)[None, :]
    order = jnp.argsort(scores, axis=1)
    return order[:, :LMAX].astype(jnp.int32)


def level_of(key, dims, cuts, smallest, high):
    factor_of, own = 1.0, jax.random.fold_in(key, 6)
    for dim, blocks in cuts:
        heights = jnp.exp(jax.random.uniform(jax.random.fold_in(own, dim), (blocks,), jnp.float32, smallest / len(cuts), high / len(cuts)))
        factor_of = factor_of * jnp.repeat(heights, dims[dim] // blocks).reshape([-1 if axis == dim else 1 for axis in range(len(dims))])
    return factor_of


def length_profile(amount, total, bound, lean):
    portions = [(1 << 20) // math.isqrt(standing ** lean) + 1 for standing in range(2, amount + 1)]
    spare, counts = total - bound - (amount - 1), [1] * (amount - 1)
    while spare > 0:
        candidates = [i for i in range(amount - 1) if counts[i] < bound]
        whole, left = sum([portions[i] for i in candidates]), spare
        for i in candidates:
            more = min(bound - counts[i], max(1, left * portions[i] // whole), spare)
            counts[i] = counts[i] + more
            spare = spare - more
    return np.array([bound] + counts)


def ragged(key, amount, total, limit, lean):
    if amount == 2:
        one = jax.random.randint(key, (), max(1, total - limit), min(limit, total - 1) + 1)
        return jnp.stack([one, total - one])
    lengths = jnp.asarray(length_profile(amount, total, limit, lean), jnp.int32)
    pairs = (amount - 1) // 2
    giver, sink = lengths[1:1 + 2 * pairs:2], lengths[2:2 + 2 * pairs:2]
    room = jnp.minimum(giver - 1, limit - sink)
    passed = jax.random.randint(jax.random.fold_in(key, 1), (pairs,), 0, 1 << 20) % (room + 1)
    lengths = lengths.at[1:1 + 2 * pairs:2].set(giver - passed).at[2:2 + 2 * pairs:2].set(sink + passed)
    return lengths[jax.random.permutation(jax.random.fold_in(key, 2), amount)]


def centred(key, dims, scale, limit, cuts=(), kind=jnp.bfloat16):
    values = jax.random.normal(key, dims, jnp.float32) * scale
    if len(cuts) > 0:
        values = level_of(key, dims, cuts, -0.22, 0.18) * values
    return jnp.clip(values, min=-limit, max=limit).astype(kind)


def setup_inputs(seed: int = 0) -> dict:
    splits = jax.random.split(jax.random.key(seed), 6)
    queries = draw_queries(jax.random.fold_in(splits[5], 71), 0)
    key_rows = draw_key_rows(jax.random.fold_in(splits[5], 71), 0)
    value_rows = centred(splits[2], (NODES, W), 1.0, 6.0, ((0, 256),))
    tile_links = draw_tile_links(jax.random.fold_in(splits[5], 71), 0)
    link_counts = ragged(splits[4], NTILES, NTILES * LMAX // 2, LMAX, 2).astype(jnp.int32)
    return dict(queries=queries, key_rows=key_rows, value_rows=value_rows, tile_links=tile_links, link_counts=link_counts)


def candidate_tiles(tile_id, slot_ids):
    device = tile_id // TPD
    group_id = device // RANKS
    range_id = device % RANKS
    within = slot_ids % TPD
    block_id = slot_ids // TPD
    offsets = jnp.array([-2, -1, 1, 2], jnp.int32)
    beside = offsets[jnp.clip(block_id - 1, 0, 3)]
    beside_range = (range_id + beside) % RANKS
    peer_group = (group_id + block_id - 4) % GROUPS
    local_tile = device * TPD + within
    beside_tile = (group_id * RANKS + beside_range) * TPD + within
    peer_tile = (peer_group * RANKS + range_id) * TPD + within
    chosen = jnp.where(block_id == 0, local_tile, jnp.where(block_id <= 4, beside_tile, peer_tile))
    return chosen.astype(jnp.int32)


def softmax_mix(query_tile, chosen_keys, chosen_values, usable):
    scores = jnp.einsum("qhd,khd->hqk", query_tile, chosen_keys) * (HD ** -0.5)
    key_mask = jnp.repeat(usable, TILE)
    scores = jnp.where(key_mask[None, None, :], scores, -jnp.inf)
    row_max = jnp.max(scores, axis=-1, keepdims=True)
    weights = jnp.exp(scores - row_max)
    row_total = jnp.sum(weights, axis=-1)
    rounded = weights.astype(jnp.bfloat16)
    mixed_rows = jnp.einsum("hqk,khd->qhd", rounded.astype(jnp.float32), chosen_values)
    return (mixed_rows / jnp.transpose(row_total)[:, :, None]).reshape(TILE, W).astype(jnp.bfloat16)


def reference(queries, key_rows, value_rows, tile_links, link_counts):
    key_tiles = key_rows.reshape(NTILES, TILE, W)
    value_tiles = value_rows.reshape(NTILES, TILE, W)

    def one_tile(tile_id):
        first = jnp.reshape(tile_id % TPD, (1,)).astype(jnp.int32)
        slot_ids = jnp.concatenate([first, tile_links[tile_id].astype(jnp.int32)])
        global_ids = candidate_tiles(tile_id, slot_ids)
        chosen_keys = key_tiles[global_ids].reshape((LMAX + 1) * TILE, H, HD).astype(jnp.float32)
        chosen_values = value_tiles[global_ids].reshape((LMAX + 1) * TILE, H, HD).astype(jnp.float32)
        query_tile = lax.dynamic_slice_in_dim(queries, (tile_id * TILE).astype(jnp.int32), TILE, 0)
        query_tile = query_tile.reshape(TILE, H, HD).astype(jnp.float32)
        usable = jnp.concatenate([jnp.ones((1,), bool), jnp.arange(LMAX, dtype=jnp.int32) < link_counts[tile_id]])
        return softmax_mix(query_tile, chosen_keys, chosen_values, usable)

    result = lax.map(one_tile, jnp.arange(NTILES, dtype=jnp.int32))
    return result.reshape(NODES, W)
```

```python
import functools
import math

import jax
import jax.numpy as jnp
from jax import lax
from jax.experimental import pallas as pl
from jax.experimental.pallas import tpu as pltpu
from jax.sharding import PartitionSpec as P

H = 16
HD = 128
LMAX = 8
TILE = 128
ROWS = 256
W = 2048
HALF = W // 2
HB = 4
BW = HB * HD
NEG = -1e30
SCALE = math.log2(math.e) / math.sqrt(HD)
PAYLOAD = 3 * HALF + 128
REPLY = HALF + 128
VMEM_LIMIT = 20 * 1024 * 1024

f32 = jnp.float32
bf16 = jnp.bfloat16


def log_multiplicity(links_ref, counts_ref, i, cand, own):
    times = jnp.int32(1 if own else 0)
    for s in range(LMAX):
        hit = (links_ref[i, s] == cand) & (s < counts_ref[i])
        times = times + hit.astype(jnp.int32)
    return jnp.where(times == 0, NEG, jnp.where(times == 1, 0.0, 1.0)).astype(f32)


def attend(q, sources, before=None, reply=None):
    ones = jnp.ones((ROWS, HD), bf16)
    scores = [
        lax.dot_general(q, k, (((1,), (1,)), ((), ())), preferred_element_type=f32)
        for k, _, _ in sources
    ]
    values = [jnp.concatenate([v, ones], axis=1) for _, v, _ in sources]
    result = []
    for i in range(2):
        rows = slice(i * TILE, (i + 1) * TILE)
        blocks = [
            [s[rows, j * TILE : (j + 1) * TILE] * SCALE + bias[i][j] for j in range(2)]
            for s, (_, _, bias) in zip(scores, sources)
        ]
        top = functools.reduce(jnp.maximum, [b for pair in blocks for b in pair])
        m = jnp.max(top, axis=1, keepdims=True)
        if before is not None:
            m = jnp.maximum(m, before[0][rows])
        if reply is not None:
            m = jnp.maximum(m, reply[1][rows])
        both = None
        for pair, v in zip(blocks, values):
            p = jnp.concatenate([jnp.exp2(b - m).astype(bf16) for b in pair], axis=1)
            part = jnp.dot(p, v, preferred_element_type=f32)
            both = part if both is None else both + part
        acc, l = both[:, :HD], both[:, HD:]
        if before is not None:
            a = jnp.exp2(before[0][rows] - m)
            acc = acc + before[2][rows] * a
            l = l + before[1][rows] * a
        if reply is not None:
            a = jnp.exp2(reply[1][rows] - m)
            acc = acc + reply[0][rows].astype(f32) * a
            l = l + a
        result.append((m, l, acc))
    return result


def both_tiles(result, which):
    return jnp.concatenate([result[0][which], result[1][which]], axis=0)


def pack_kernel(links_ref, counts_ref, q_ref, k_ref, v_ref, a_ref, b_ref):
    i = pl.program_id(0) // 2
    g = lax.axis_index("group")
    even = (g % 2) == 0
    lane = lax.broadcasted_iota(jnp.int32, (64, 128), 1)
    near_a = jnp.where(even, 5, 7)
    near_b = jnp.where(even, 7, 5)
    for ref, near, kv, qs in ((a_ref, near_a, 0, HALF), (b_ref, near_b, HALF, 0)):
        ref[:, 0:HALF] = k_ref[:, kv : kv + HALF]
        ref[:, HALF : 2 * HALF] = v_ref[:, kv : kv + HALF]
        ref[:, 2 * HALF : 3 * HALF] = q_ref[:, qs : qs + HALF]
        extra = jnp.zeros((64, 128), f32)
        for n, cand in enumerate((near * 2, near * 2 + 1, 12, 13)):
            bias = log_multiplicity(links_ref, counts_ref, i, cand, False)
            extra = jnp.where(lane == n, bias, extra)
        ref[:, 3 * HALF :] = extra.astype(bf16)


def pack(links, counts, q, k, v):
    rows = pl.BlockSpec((64, W), lambda s: (s, 0))
    out = pl.BlockSpec((64, PAYLOAD), lambda s: (s, 0))
    smem = pl.BlockSpec(memory_space=pltpu.SMEM)
    return pl.pallas_call(
        pack_kernel,
        grid=(4,),
        in_specs=[smem, smem, rows, rows, rows],
        out_specs=[out, out],
        out_shape=[jax.ShapeDtypeStruct((ROWS, PAYLOAD), bf16)] * 2,
        compiler_params=pltpu.CompilerParams(vmem_limit_bytes=VMEM_LIMIT),
        cost_estimate=pl.CostEstimate(flops=0, bytes_accessed=6 * 1024 * 1024, transcendentals=0),
        name="pack",
    )(links, counts, q, k, v)


def remote_kernel(q_ref, bias_ref, k0_ref, v0_ref, k1_ref, v1_ref, out_ref):
    step = pl.program_id(0)
    lane = lax.broadcasted_iota(jnp.int32, (ROWS, 128), 1)
    bias = [
        [
            [
                jnp.broadcast_to(
                    bias_ref[i * TILE : (i + 1) * TILE, 2 * s + j : 2 * s + j + 1].astype(f32),
                    (TILE, TILE),
                )
                for j in range(2)
            ]
            for i in range(2)
        ]
        for s in range(2)
    ]
    stats = jnp.zeros((ROWS, 128), f32)
    rows_out = []
    for h in range(HB):
        c = slice(h * HD, (h + 1) * HD)
        done = attend(
            q_ref[:, c],
            [(k0_ref[:, c], v0_ref[:, c], bias[0]), (k1_ref[:, c], v1_ref[:, c], bias[1])],
        )
        m, l, acc = (both_tiles(done, n) for n in range(3))
        rows_out.append((acc / l).astype(bf16))
        total = m + jnp.log2(l)
        high = total.astype(bf16).astype(f32)
        rest = total - high
        middle = rest.astype(bf16).astype(f32)
        low = rest - middle
        for n, piece in enumerate((high, middle, low)):
            stats = jnp.where(lane == 3 * h + n, piece, stats)
    block = jnp.concatenate(rows_out, axis=1)
    stats = stats.astype(bf16)

    @pl.when(step == 0)
    def _():
        out_ref[:, 0:BW] = block
        out_ref[:, 2 * BW :] = stats

    @pl.when(step == 1)
    def _():
        out_ref[:, BW : 2 * BW] = block
        moved = pltpu.roll(stats.astype(f32), 64, 1)
        out_ref[:, 2 * BW :] = jnp.where(
            lane < 64, out_ref[:, 2 * BW :].astype(f32), moved
        ).astype(bf16)


def remote(asked, k, v, other, half):
    first = half * 2
    cost = 2 * 2 * 2 * ROWS * ROWS * HALF
    return pl.pallas_call(
        remote_kernel,
        grid=(2,),
        in_specs=[
            pl.BlockSpec((ROWS, BW), lambda s: (0, 4 + s)),
            pl.BlockSpec((ROWS, 128), lambda s: (0, 3 * HALF // 128)),
            pl.BlockSpec((ROWS, BW), lambda s: (0, first + s)),
            pl.BlockSpec((ROWS, BW), lambda s: (0, first + s)),
            pl.BlockSpec((ROWS, BW), lambda s: (0, s)),
            pl.BlockSpec((ROWS, BW), lambda s: (0, 2 + s)),
        ],
        out_specs=pl.BlockSpec((ROWS, REPLY), lambda s: (0, 0)),
        out_shape=jax.ShapeDtypeStruct((ROWS, REPLY), bf16),
        compiler_params=pltpu.CompilerParams(vmem_limit_bytes=VMEM_LIMIT),
        cost_estimate=pl.CostEstimate(
            flops=cost, bytes_accessed=3 * 1024 * 1024, transcendentals=ROWS * ROWS * H
        ),
        name="remote",
    )(asked, asked, k, v, other, other)


def local_kernel(plan, has_before, has_reply, last, *refs):
    refs = list(refs)
    links_ref, counts_ref = refs.pop(0), refs.pop(0)
    q_ref = refs.pop(0)
    step = pl.program_id(0)
    g = lax.axis_index("group")
    odd_core = (lax.axis_index("rank") % 2) == 1
    odd_group = (g % 2) == 1
    sources = []
    for role in plan:
        if role == "pairs":
            ka, va, kb, vb = (refs.pop(0) for _ in range(4))
            first_half = step < 2
            k = jnp.where(first_half, ka[...], kb[...])
            v = jnp.where(first_half, va[...], vb[...])
            block = jnp.where(first_half != odd_group, 5, 7)
        else:
            k, v = refs.pop(0)[...], refs.pop(0)[...]
            block = {
                "own": 0,
                "core": jnp.where(odd_core, 2, 3),
                "relay": jnp.where(odd_core, 3, 2),
                "minus": 1,
                "plus": 4,
            }[role]
        bias = [
            [
                log_multiplicity(links_ref, counts_ref, i, block * 2 + j, role == "own" and i == j)
                for j in range(2)
            ]
            for i in range(2)
        ]
        sources.append((k, v, bias))
    if has_before:
        acc_in, ml_in = refs.pop(0), refs.pop(0)
    if has_reply:
        rows_a, stats_a, rows_b, stats_b = (refs.pop(0) for _ in range(4))
        first_half = step < 2
        rows_in = jnp.where(first_half, rows_a[...], rows_b[...])
        stats_in = jnp.where(first_half, stats_a[...].astype(f32), stats_b[...].astype(f32))
        stats_in = jnp.where(step % 2 == 0, stats_in, pltpu.roll(stats_in, 64, 1))
    lane = lax.broadcasted_iota(jnp.int32, (ROWS, 128), 1)
    stats = jnp.zeros((ROWS, 128), f32)
    for h in range(HB):
        c = slice(h * HD, (h + 1) * HD)
        before = reply = None
        if has_before:
            ml = ml_in[...]
            before = (
                ml[:, 2 * h : 2 * h + 1],
                jnp.broadcast_to(ml[:, 2 * h + 1 : 2 * h + 2], (ROWS, HD)),
                acc_in[:, c],
            )
        if has_reply:
            total = (
                stats_in[:, 3 * h : 3 * h + 1]
                + stats_in[:, 3 * h + 1 : 3 * h + 2]
                + stats_in[:, 3 * h + 2 : 3 * h + 3]
            )
            reply = (rows_in[:, c], total)
        done = attend(q_ref[:, c], [(k[:, c], v[:, c], b) for k, v, b in sources], before, reply)
        m, l, acc = (both_tiles(done, n) for n in range(3))
        if last:
            refs[0][:, c] = (acc / l).astype(bf16)
        else:
            refs[0][:, c] = acc
            stats = jnp.where(lane == 2 * h, m, stats)
            stats = jnp.where(lane == 2 * h + 1, l, stats)
    if not last:
        refs[1][...] = stats


def local(links, counts, q, sources, before=None, reply=None, last=False):
    has_reply = reply is not None
    smem = pl.BlockSpec(memory_space=pltpu.SMEM)
    part = lambda row, at: pl.BlockSpec((ROWS, BW), lambda s: (row, at(s)))
    low = lambda s: jnp.minimum(s, 1)
    high = lambda s: jnp.maximum(s - 2, 0)
    straight = lambda s: s
    specs, args, plan = [smem, smem, part(0, straight)], [links, counts, q], []
    for role, arrays in sources:
        plan.append(role)
        if role == "own":
            specs += [part(0, straight)] * 2
            args += list(arrays)
        elif role == "pairs":
            a, b = arrays
            specs += [part(0, low), part(0, lambda s: 2 + low(s))]
            specs += [part(0, high), part(0, lambda s: 2 + high(s))]
            args += [a, a, b, b]
        else:
            specs += [part(0, straight), part(1, straight)]
            args += [arrays, arrays]
    stat = pl.BlockSpec((ROWS, 128), lambda s: (0, s))
    if before is not None:
        specs += [part(0, straight), stat]
        args += list(before)
    if reply is not None:
        a, b = reply
        tail = pl.BlockSpec((ROWS, 128), lambda s: (0, HALF // 128))
        specs += [part(0, low), tail, part(0, high), tail]
        args += [a, a, b, b]
    if last:
        out_specs = part(0, straight)
        out_shape = jax.ShapeDtypeStruct((ROWS, W), bf16)
    else:
        out_specs = [part(0, straight), stat]
        out_shape = [
            jax.ShapeDtypeStruct((ROWS, W), f32),
            jax.ShapeDtypeStruct((ROWS, 4 * 128), f32),
        ]
    return pl.pallas_call(
        functools.partial(local_kernel, tuple(plan), before is not None, has_reply, last),
        grid=(4,),
        in_specs=specs,
        out_specs=out_specs,
        out_shape=out_shape,
        compiler_params=pltpu.CompilerParams(vmem_limit_bytes=VMEM_LIMIT),
        cost_estimate=pl.CostEstimate(
            flops=(400 if has_reply else 4) * ROWS * ROWS * W * len(plan),
            bytes_accessed=(2 + 2 * len(plan)) * 1024 * 1024,
            transcendentals=ROWS * ROWS * H * len(plan),
        ),
        name="local_" + "_".join(plan),
    )(*args)


def shards(q, k, v, links, counts):
    ranks = lax.axis_size("rank")
    along = lambda x, d: lax.ppermute(x, "rank", [(i, (i + d) % ranks) for i in range(ranks)])
    core = lambda x: lax.ppermute(x, "rank", [(i, i ^ 1) for i in range(ranks)])
    to_a = lambda x: lax.ppermute(x, "group", [(i, i ^ 1) for i in range(4)])
    to_b = lambda x: lax.ppermute(x, "group", [(i, 3 - i) for i in range(4)])

    kv = jnp.concatenate([k, v], axis=0)
    pay_a, pay_b = pack(links, counts, q, k, v)
    from_minus = along(kv, 2)
    from_plus = along(kv, -2)
    got_a = to_a(pay_a)
    got_b = to_b(pay_b)
    from_core = core(kv)
    state = local(links, counts, q, [("own", (k, v)), ("core", from_core)])

    got_a, got_b, state = lax.optimization_barrier((got_a, got_b, state))
    part_a = remote(got_a, k, v, got_b, 1)
    back_a = to_a(part_a)
    part_b = remote(got_b, k, v, got_a, 0)
    back_b = to_b(part_b)
    got_a, got_b, part_a, part_b = lax.optimization_barrier((got_a, got_b, part_a, part_b))
    state = local(links, counts, q, [("pairs", (got_a, got_b))], state)

    from_minus, from_plus, state = lax.optimization_barrier((from_minus, from_plus, state))
    odd = (lax.axis_index("rank") % 2) == 1
    relay = core(jnp.where(odd, from_minus, from_plus))
    near = [("minus", from_minus), ("plus", from_plus)]
    state = local(links, counts, q, near, state, (back_b, back_a))
    return local(links, counts, q, [("relay", relay)], state, None, True)


def solution(mesh):
    rows = P(("group", "rank"), None)
    return jax.shard_map(
        shards,
        mesh=mesh,
        in_specs=(rows, rows, rows, rows, P(("group", "rank"))),
        out_specs=rows,
        check_vma=False,
    )
```

```python
import functools
import math

import jax
import jax.numpy as jnp
from jax import lax
from jax.experimental import pallas as pl
from jax.experimental.pallas import tpu as pltpu
from jax.sharding import PartitionSpec as P

H = 16
HD = 128
LMAX = 8
TILE = 128
ROWS = 256
W = 2048
HALF = W // 2
NEG = -1e30
SCALE = math.log2(math.e) / math.sqrt(HD)
PAYLOAD = 3 * ROWS + 16
REPLY = HALF + 32
PACK_LIMIT = 20 * 1024 * 1024
VMEM_LIMIT = 20 * 1024 * 1024

f32 = jnp.float32
bf16 = jnp.bfloat16


def log_multiplicity(links_ref, counts_ref, i, cand, own):
    times = jnp.int32(1 if own else 0)
    for s in range(LMAX):
        hit = (links_ref[i, s] == cand) & (s < counts_ref[i])
        times = times + hit.astype(jnp.int32)
    return jnp.where(times == 0, NEG, jnp.where(times == 1, 0.0, 1.0)).astype(f32)


def bias_row(left, right):
    lane = lax.broadcasted_iota(jnp.int32, (1, ROWS), 1)
    return jnp.where(lane < TILE, left, right)


def score(q, sources):
    raw, tops = [], []
    for k, _, bias in sources:
        s = lax.dot_general(k, q, (((1,), (1,)), ((), ())), preferred_element_type=f32)
        for j in range(2):
            block = s[j * TILE : (j + 1) * TILE]
            raw.append((block, bias[j]))
            tops.append(jnp.max(block, axis=0, keepdims=True) * SCALE + bias[j])
    return raw, tops


def weigh(scored, before=None, reply=None):
    raw, tops = scored
    if before is not None:
        tops = tops + [before[0]]
    if reply is not None:
        tops = tops + [reply[1]]
    m = functools.reduce(jnp.maximum, tops)
    p = [jnp.exp2(block * SCALE + (bias - m)).astype(bf16) for block, bias in raw]
    return m, jnp.concatenate(p, axis=0)


def mix(weighed, sources, before=None, reply=None):
    m, p = weighed
    values = jnp.concatenate([v.T for _, v, _ in sources], axis=1)
    values = jnp.concatenate([values, jnp.ones((16, values.shape[1]), bf16)], axis=0)
    both = jnp.dot(values, p, preferred_element_type=f32)
    acc, l = both[:HD], both[HD : HD + 1]
    if before is not None:
        a = jnp.exp2(before[0] - m)
        acc = acc + before[2] * a
        l = l + before[1] * a
    if reply is not None:
        a = jnp.exp2(reply[1] - m)
        acc = acc + reply[0].astype(f32) * a
        l = l + a
    return m, l, acc


def over_heads(heads, load, store):
    held, scored, weighed = {}, {}, {}
    for t in range(heads + 2):
        if t < heads:
            held[t] = load(t)
            scored[t] = score(*held[t][:2])
        if 0 <= t - 1 < heads:
            weighed[t - 1] = weigh(scored.pop(t - 1), *held[t - 1][2:])
        if t >= 2:
            _, sources, before, reply = held.pop(t - 2)
            store(t - 2, *mix(weighed.pop(t - 2), sources, before, reply))


def pack_kernel(links_ref, counts_ref, q_hbm, k_hbm, v_hbm, kv_ref, a_ref, b_ref, table_ref, sems):
    g = lax.axis_index("group")
    even = (g % 2) == 0
    copies = []

    def begin(src, dst):
        copies.append(pltpu.make_async_copy(src, dst, sems.at[len(copies)]))
        copies[-1].start()

    begin(k_hbm, kv_ref.at[pl.ds(0, ROWS)])
    begin(v_hbm, kv_ref.at[pl.ds(ROWS, ROWS)])
    begin(q_hbm.at[:, pl.ds(HALF, HALF)], a_ref.at[pl.ds(2 * ROWS, ROWS)])
    begin(q_hbm.at[:, pl.ds(0, HALF)], b_ref.at[pl.ds(2 * ROWS, ROWS)])
    for i in range(2):
        for c in range(16):
            table_ref[i, c] = log_multiplicity(links_ref, counts_ref, i, c, c == i)
    row = lax.broadcasted_iota(jnp.int32, (16, 128), 0)
    for ref, near in ((a_ref, jnp.where(even, 5, 7)), (b_ref, jnp.where(even, 7, 5))):
        extra = jnp.zeros((16, 128), f32)
        for i in range(2):
            for n, cand in enumerate((near * 2, near * 2 + 1, 12, 13)):
                extra = jnp.where(row == 4 * i + n, table_ref[i, cand], extra)
        ref[3 * ROWS :, 0:128] = extra.astype(bf16)
        ref[3 * ROWS :, 128:] = jnp.zeros((16, HALF - 128), bf16)
    copies[0].wait()
    for ref, at in ((a_ref, 0), (b_ref, HALF)):
        ref[0:ROWS] = kv_ref[0:ROWS, at : at + HALF]
    copies[1].wait()
    for ref, at in ((a_ref, 0), (b_ref, HALF)):
        ref[ROWS : 2 * ROWS] = kv_ref[ROWS:, at : at + HALF]
    copies[2].wait()
    copies[3].wait()


def pack(links, counts, q, k, v):
    smem = pl.BlockSpec(memory_space=pltpu.SMEM)
    vmem = pl.BlockSpec(memory_space=pltpu.VMEM)
    hbm = pl.BlockSpec(memory_space=pltpu.HBM)
    return pl.pallas_call(
        pack_kernel,
        in_specs=[smem, smem, hbm, hbm, hbm],
        out_specs=[vmem, vmem, vmem, smem],
        out_shape=[
            jax.ShapeDtypeStruct((2 * ROWS, W), bf16),
            jax.ShapeDtypeStruct((PAYLOAD, HALF), bf16),
            jax.ShapeDtypeStruct((PAYLOAD, HALF), bf16),
            jax.ShapeDtypeStruct((2, 16), f32),
        ],
        scratch_shapes=[pltpu.SemaphoreType.DMA((4,))],
        compiler_params=pltpu.CompilerParams(vmem_limit_bytes=PACK_LIMIT),
        cost_estimate=pl.CostEstimate(flops=0, bytes_accessed=8 * 1024 * 1024, transcendentals=0),
        name="pack",
    )(links, counts, q, k, v)


def remote_kernel(half, asked_ref, kv_ref, other_ref, out_ref):
    extra = asked_ref[3 * ROWS :, 0:128].astype(f32)
    bias = [
        jnp.concatenate([extra[n : n + 1], extra[4 + n : 5 + n]], axis=1) for n in range(4)
    ]
    stats = [[], [], []]

    def load(h):
        c = slice(h * HD, (h + 1) * HD)
        own = slice(half * HALF + h * HD, half * HALF + (h + 1) * HD)
        sources = [
            (kv_ref[0:ROWS, own], kv_ref[ROWS:, own], bias[0:2]),
            (other_ref[0:ROWS, c], other_ref[ROWS : 2 * ROWS, c], bias[2:4]),
        ]
        return asked_ref[2 * ROWS : 3 * ROWS, c], sources, None, None

    def store(h, m, l, acc):
        out_ref[h * HD : (h + 1) * HD] = (acc / l).astype(bf16)
        total = m + jnp.log2(l)
        high = total.astype(bf16).astype(f32)
        rest = total - high
        middle = rest.astype(bf16).astype(f32)
        for rows, piece in zip(stats, (high, middle, rest - middle)):
            rows.append(piece)

    over_heads(H // 2, load, store)
    pieces = [jnp.concatenate(rows, axis=0) for rows in stats]
    pieces.append(jnp.zeros_like(pieces[0]))
    out_ref[HALF:] = jnp.concatenate(pieces, axis=0).astype(bf16)


def remote(asked, kv, other, half):
    vmem = pl.BlockSpec(memory_space=pltpu.VMEM)
    return pl.pallas_call(
        functools.partial(remote_kernel, half),
        in_specs=[vmem] * 3,
        out_specs=vmem,
        out_shape=jax.ShapeDtypeStruct((REPLY, ROWS), bf16),
        compiler_params=pltpu.CompilerParams(vmem_limit_bytes=VMEM_LIMIT),
        cost_estimate=pl.CostEstimate(
            flops=800 * ROWS * ROWS * HALF,
            bytes_accessed=1024 * 1024,
            transcendentals=ROWS * ROWS * H,
        ),
        name="remote",
    )(asked, kv, other)


def local_kernel(plan, has_before, has_reply, last, *refs):
    refs = list(refs)
    table_ref, q_ref = refs.pop(0), refs.pop(0)
    odd_core = (lax.axis_index("rank") % 2) == 1
    odd_group = (lax.axis_index("group") % 2) == 1
    sources = []
    for role in plan:
        if role == "pairs":
            arrays = (refs.pop(0), refs.pop(0))
            blocks = (jnp.where(odd_group, 7, 5), jnp.where(odd_group, 5, 7))
        else:
            arrays = refs.pop(0)
            block = {
                "own": 0,
                "core": jnp.where(odd_core, 2, 3),
                "relay": jnp.where(odd_core, 3, 2),
                "first": jnp.where(odd_core, 1, 4),
                "second": jnp.where(odd_core, 4, 1),
            }[role]
            blocks = (block, block)
        bias = [
            [bias_row(table_ref[0, block * 2 + j], table_ref[1, block * 2 + j]) for j in range(2)]
            for block in blocks
        ]
        sources.append((role, arrays, bias))
    if has_before:
        acc_in, ml_in = refs.pop(0), refs.pop(0)
    if has_reply:
        reply_refs = (refs.pop(0), refs.pop(0))
        totals = []
        for ref in reply_refs:
            tail = ref[HALF:].astype(f32)
            totals.append(tail[0:8] + tail[8:16] + tail[16:24])
    tops, sums, copies = [], [], []

    def load(h):
        half, inner = h // (H // 2), h % (H // 2)
        c = slice(h * HD, (h + 1) * HD)
        low = slice(inner * HD, (inner + 1) * HD)
        given = []
        for role, arrays, bias in sources:
            array, at = (arrays[half], low) if role == "pairs" else (arrays, c)
            given.append((array[0:ROWS, at], array[ROWS : 2 * ROWS, at], bias[half]))
        before = reply = None
        if has_before:
            before = (ml_in[h : h + 1], ml_in[H + h : H + h + 1], acc_in[c])
        if has_reply:
            reply = (reply_refs[half][low], totals[half][inner : inner + 1])
        return q_ref[:, c], given, before, reply

    def store(h, m, l, acc):
        c = slice(h * HD, (h + 1) * HD)
        if last:
            out_hbm, out_ref, sems = refs
            out_ref[:, c] = (acc / l).astype(bf16).T
            if h % 2 == 1:
                n, pair = h // 2, slice((h - 1) * HD, (h + 1) * HD)
                copies.append(
                    pltpu.make_async_copy(out_ref.at[:, pair], out_hbm.at[:, pair], sems.at[n])
                )
                copies[-1].start()
        else:
            refs[0][c] = acc
            tops.append(m)
            sums.append(l)

    over_heads(H, load, store)
    for copy in copies:
        copy.wait()
    if not last:
        refs[1][...] = jnp.concatenate(tops + sums, axis=0)


def local(table, q, sources, before=None, reply=None, last=False):
    vmem = pl.BlockSpec(memory_space=pltpu.VMEM)
    plan = tuple(role for role, _ in sources)
    args = [table, q]
    for role, arrays in sources:
        args += list(arrays) if role == "pairs" else [arrays]
    args += list(before or ()) + list(reply or ())
    if last:
        out_specs = pl.BlockSpec(memory_space=pl.ANY)
        out_shape = jax.ShapeDtypeStruct((ROWS, W), bf16)
        scratch = [pltpu.VMEM((ROWS, W), bf16), pltpu.SemaphoreType.DMA((H // 2,))]
    else:
        scratch = []
        out_specs = [vmem, vmem]
        out_shape = [
            jax.ShapeDtypeStruct((W, ROWS), f32),
            jax.ShapeDtypeStruct((2 * H, ROWS), f32),
        ]
    return pl.pallas_call(
        functools.partial(local_kernel, plan, before is not None, reply is not None, last),
        in_specs=[pl.BlockSpec(memory_space=pltpu.SMEM)] + [vmem] * (len(args) - 1),
        out_specs=out_specs,
        out_shape=out_shape,
        scratch_shapes=scratch,
        compiler_params=pltpu.CompilerParams(vmem_limit_bytes=VMEM_LIMIT),
        cost_estimate=pl.CostEstimate(
            flops=4 * ROWS * ROWS * W, bytes_accessed=1024 * 1024, transcendentals=0
        ),
        name="local_" + "_".join(plan),
    )(*args)


def shards(q, k, v, links, counts):
    ranks = lax.axis_size("rank")
    across = lambda x, to: lax.ppermute(x, "rank", [(i, to(i) % ranks) for i in range(ranks)])
    in_hbm = lambda x: pltpu.with_memory_space_constraint(x, pltpu.HBM)
    core = lambda x: across(x, lambda i: i ^ 1)
    to_a = lambda x: lax.ppermute(x, "group", [(i, i ^ 1) for i in range(4)])
    to_b = lambda x: lax.ppermute(x, "group", [(i, 3 - i) for i in range(4)])

    kv, pay_a, pay_b, table = pack(links, counts, *(in_hbm(x) for x in (q, k, v)))
    got_a = to_a(pay_a)
    got_b = to_b(pay_b)
    first = across(kv, lambda i: i + 2 if i % 2 else i - 2)
    from_core = core(kv)
    state = local(table, q, [("own", kv), ("core", from_core)])

    first, state = lax.optimization_barrier((first, state))
    kv_later, first = lax.optimization_barrier((kv, first))
    second = across(kv_later, lambda i: i - 2 if i % 2 else i + 2)
    relay = core(first)

    got_a, got_b, _ = lax.optimization_barrier((got_a, got_b, kv_later))
    part_a = remote(got_a, kv, got_b, 1)
    back_a = to_a(part_a)
    part_b = remote(got_b, kv, got_a, 0)
    back_b = to_b(part_b)
    got_a, got_b, part_a, part_b = lax.optimization_barrier((got_a, got_b, part_a, part_b))
    middle = [("first", first), ("relay", relay), ("pairs", (got_a, got_b))]
    state = local(table, q, middle, state)
    second, state = lax.optimization_barrier((second, state))
    return local(table, q, [("second", second)], state, (back_b, back_a), True)


def solution(mesh):
    rows = P(("group", "rank"), None)
    return jax.shard_map(
        shards,
        mesh=mesh,
        in_specs=(rows, rows, rows, rows, P(("group", "rank"))),
        out_specs=rows,
        check_vma=False,
    )
```

```python
import functools
import math

import jax
import jax.numpy as jnp
from jax import lax
from jax.experimental import pallas as pl
from jax.experimental.pallas import tpu as pltpu
from jax.sharding import PartitionSpec as P

H = 16
HD = 128
LMAX = 8
TILE = 128
ROWS = 256
W = 2048
HALF = W // 2
NEG = -1e30
SCALE = math.log2(math.e) / math.sqrt(HD)
PARTS = 2
PH = H // 2 // PARTS
PW = PH * HD
PAYLOAD = 3 * ROWS + 16
REPLY = PW + 16
SPLIT = 4
VMEM_LIMIT = 20 * 1024 * 1024
REMOTE_COST = 200

f32 = jnp.float32
bf16 = jnp.bfloat16


def log_multiplicity(links_ref, counts_ref, i, cand, own):
    times = jnp.int32(1 if own else 0)
    for s in range(LMAX):
        hit = (links_ref[i, s] == cand) & (s < counts_ref[i])
        times = times + hit.astype(jnp.int32)
    return jnp.where(times == 0, NEG, jnp.where(times == 1, 0.0, 1.0)).astype(f32)


def score(q, sources):
    raw, tops = [], []
    for k, _, bias in sources:
        s = lax.dot_general(k, q, (((1,), (1,)), ((), ())), preferred_element_type=f32)
        for j in range(2):
            block = s[j * TILE : (j + 1) * TILE]
            raw.append((block, bias[j]))
            tops.append(jnp.max(block, axis=0, keepdims=True) * SCALE + bias[j])
    return raw, tops


def weigh(scored, before=None, reply=None):
    raw, tops = scored
    if before is not None:
        tops = tops + [before[0]]
    if reply is not None:
        tops = tops + [reply[1]]
    m = functools.reduce(jnp.maximum, tops)
    p = [jnp.exp2(block * SCALE + (bias - m)).astype(bf16) for block, bias in raw]
    return m, jnp.concatenate(p, axis=0)


def mix(weighed, sources, before=None, reply=None):
    m, p = weighed
    values = jnp.concatenate([v.T for _, v, _ in sources], axis=1)
    values = jnp.concatenate([values, jnp.ones((16, values.shape[1]), bf16)], axis=0)
    both = jnp.dot(values, p, preferred_element_type=f32)
    acc, l = both[:HD], both[HD : HD + 1]
    if before is not None:
        a = jnp.exp2(before[0] - m)
        acc = acc + before[2] * a
        l = l + before[1] * a
    if reply is not None:
        a = jnp.exp2(reply[1] - m)
        acc = acc + reply[0].astype(f32) * a
        l = l + a
    return m, l, acc


def over_heads(heads, load, store):
    held, scored, weighed = {}, {}, {}
    for t in range(heads + 2):
        if t < heads:
            held[t] = load(t)
            scored[t] = score(*held[t][:2])
        if 0 <= t - 1 < heads:
            weighed[t - 1] = weigh(scored.pop(t - 1), *held[t - 1][2:])
        if t >= 2:
            _, sources, before, reply = held.pop(t - 2)
            store(t - 2, *mix(weighed.pop(t - 2), sources, before, reply))


def payload_heads(way, part):
    return way * HALF + part * PW, (1 - way) * HALF + part * PW


def pack_kernel(links_hbm, counts_hbm, q_hbm, k_hbm, v_hbm, kv_ref, *refs):
    pay_refs, table_ref = refs[: 2 * PARTS], refs[2 * PARTS]
    links_ref, counts_ref, small_sems, sems = refs[2 * PARTS + 1 :]
    small = [
        pltpu.make_async_copy(links_hbm, links_ref, small_sems.at[0]),
        pltpu.make_async_copy(counts_hbm, counts_ref, small_sems.at[1]),
    ]
    for copy in small:
        copy.start()
    copies = []

    def begin(src, dst):
        copies.append(pltpu.make_async_copy(src, dst, sems.at[len(copies)]))
        copies[-1].start()

    step = ROWS // SPLIT
    for n, hbm in enumerate((k_hbm, v_hbm)):
        for i in range(SPLIT):
            begin(hbm.at[pl.ds(i * step, step)], kv_ref.at[pl.ds(n * ROWS + i * step, step)])
    for n, ref in enumerate(pay_refs):
        column = payload_heads(n // PARTS, n % PARTS)[1]
        begin(q_hbm.at[:, pl.ds(column, PW)], ref.at[pl.ds(2 * ROWS, ROWS)])
    for copy in small:
        copy.wait()
    bias = [
        [log_multiplicity(links_ref, counts_ref, i, c, c == i) for i in range(2)]
        for c in range(16)
    ]
    lane = lax.broadcasted_iota(jnp.int32, (16, ROWS), 1)
    row = lax.broadcasted_iota(jnp.int32, (16, ROWS), 0)
    table = jnp.zeros((16, ROWS), f32)
    for c in range(16):
        table = jnp.where(row == c, jnp.where(lane < TILE, bias[c][0], bias[c][1]), table)
    table_ref[...] = table
    even = (lax.axis_index("group") % 2) == 0
    row = lax.broadcasted_iota(jnp.int32, (16, 128), 0)
    for way in range(2):
        extra = jnp.zeros((16, 128), f32)
        for i in range(2):
            for j in range(2):
                one, three = bias[10 + j][i], bias[14 + j][i]
                near = jnp.where(even, one, three) if way == 0 else jnp.where(even, three, one)
                extra = jnp.where(row == 4 * i + j, near, extra)
                extra = jnp.where(row == 4 * i + 2 + j, bias[12 + j][i], extra)
        for ref in pay_refs[way * PARTS : (way + 1) * PARTS]:
            ref[3 * ROWS :, 0:128] = extra.astype(bf16)
            ref[3 * ROWS :, 128:] = jnp.zeros((16, PW - 128), bf16)
    for part in range(2 * SPLIT):
        copies[part].wait()
        rows = slice(part * step, (part + 1) * step)
        for n, ref in enumerate(pay_refs):
            column = payload_heads(n // PARTS, n % PARTS)[0]
            ref[rows] = kv_ref[rows, column : column + PW]
    for copy in copies[2 * SPLIT :]:
        copy.wait()


def pack(links, counts, q, k, v):
    vmem = pl.BlockSpec(memory_space=pltpu.VMEM)
    hbm = pl.BlockSpec(memory_space=pltpu.HBM)
    args = [pltpu.with_memory_space_constraint(x, pltpu.HBM) for x in (links, counts, q, k, v)]
    out = pl.pallas_call(
        pack_kernel,
        in_specs=[hbm] * 5,
        out_specs=[vmem] * (2 + 2 * PARTS),
        out_shape=[jax.ShapeDtypeStruct((2 * ROWS, W), bf16)]
        + [jax.ShapeDtypeStruct((PAYLOAD, PW), bf16)] * (2 * PARTS)
        + [jax.ShapeDtypeStruct((16, ROWS), f32)],
        scratch_shapes=[
            pltpu.SMEM((2, LMAX), jnp.int32),
            pltpu.SMEM((2,), jnp.int32),
            pltpu.SemaphoreType.DMA((2,)),
            pltpu.SemaphoreType.DMA((2 * SPLIT + 2 * PARTS,)),
        ],
        compiler_params=pltpu.CompilerParams(vmem_limit_bytes=VMEM_LIMIT),
        cost_estimate=pl.CostEstimate(flops=0, bytes_accessed=8 * 1024 * 1024, transcendentals=0),
        name="pack",
    )(*args)
    return out[0], out[1 : 1 + PARTS], out[1 + PARTS : 1 + 2 * PARTS], out[-1]


def remote_kernel(part, kv_ref, a_ref, b_ref, out_a, out_b):
    asked, other, outs = (a_ref, b_ref), (b_ref, a_ref), (out_a, out_b)
    bias, stats = [], []
    for way in range(2):
        extra = asked[way][3 * ROWS :, 0:128].astype(f32)
        bias.append(
            [jnp.concatenate([extra[n : n + 1], extra[4 + n : 5 + n]], axis=1) for n in range(4)]
        )
        stats.append([[], [], []])

    def load(h):
        way, inner = h // PH, h % PH
        c = slice(inner * HD, (inner + 1) * HD)
        first = payload_heads(way, part)[1] + inner * HD
        own = slice(first, first + HD)
        sources = [
            (kv_ref[0:ROWS, own], kv_ref[ROWS:, own], bias[way][0:2]),
            (other[way][0:ROWS, c], other[way][ROWS : 2 * ROWS, c], bias[way][2:4]),
        ]
        return asked[way][2 * ROWS : 3 * ROWS, c], sources, None, None

    def store(h, m, l, acc):
        way, inner = h // PH, h % PH
        outs[way][inner * HD : (inner + 1) * HD] = (acc / l).astype(bf16)
        total = m + jnp.log2(l)
        high = total.astype(bf16).astype(f32)
        rest = total - high
        middle = rest.astype(bf16).astype(f32)
        for rows, piece in zip(stats[way], (high, middle, rest - middle)):
            rows.append(piece)

    over_heads(2 * PH, load, store)
    for way in range(2):
        rows = stats[way][0] + stats[way][1] + stats[way][2]
        rows += [jnp.zeros((1, ROWS), f32)] * (16 - len(rows))
        outs[way][PW:] = jnp.concatenate(rows, axis=0).astype(bf16)


def remote(kv, a, b, part):
    vmem = pl.BlockSpec(memory_space=pltpu.VMEM)
    return pl.pallas_call(
        functools.partial(remote_kernel, part),
        in_specs=[vmem] * 3,
        out_specs=[vmem] * 2,
        out_shape=[jax.ShapeDtypeStruct((REPLY, ROWS), bf16)] * 2,
        compiler_params=pltpu.CompilerParams(vmem_limit_bytes=VMEM_LIMIT),
        cost_estimate=pl.CostEstimate(
            flops=REMOTE_COST * ROWS * ROWS * HALF, bytes_accessed=1024 * 1024, transcendentals=0
        ),
        name=f"remote_{part}",
    )(kv, a, b)


def local_kernel(plan, has_before, has_reply, last, *refs):
    refs = list(refs)
    table_ref, q_ref = refs.pop(0), refs.pop(0)
    odd_core = (lax.axis_index("rank") % 2) == 1
    odd_group = (lax.axis_index("group") % 2) == 1
    sources = []
    for role in plan:
        if role == "pairs":
            arrays = [refs.pop(0) for _ in range(2 * PARTS)]
            blocks = (jnp.where(odd_group, 7, 5), jnp.where(odd_group, 5, 7))
        else:
            arrays = refs.pop(0)
            block = {
                "own": 0,
                "core": jnp.where(odd_core, 2, 3),
                "relay": jnp.where(odd_core, 3, 2),
                "first": jnp.where(odd_core, 1, 4),
                "second": jnp.where(odd_core, 4, 1),
            }[role]
            blocks = (block, block)
        bias = [
            [table_ref[pl.ds(block * 2 + j, 1), :] for j in range(2)] for block in blocks
        ]
        sources.append((role, arrays, bias))
    if has_before:
        acc_in, ml_in = refs.pop(0), refs.pop(0)
    if has_reply:
        reply_refs = [refs.pop(0) for _ in range(2 * PARTS)]
        totals = []
        for ref in reply_refs:
            tail = ref[PW:].astype(f32)
            totals.append(tail[0:PH] + tail[PH : 2 * PH] + tail[2 * PH : 3 * PH])
    tops, sums, copies = [], [], []

    def load(h):
        piece, inner = h // PH, h % PH
        half = h // (H // 2)
        c = slice(h * HD, (h + 1) * HD)
        low = slice(inner * HD, (inner + 1) * HD)
        given = []
        for role, arrays, bias in sources:
            array, at = (arrays[piece], low) if role == "pairs" else (arrays, c)
            given.append((array[0:ROWS, at], array[ROWS : 2 * ROWS, at], bias[half]))
        before = reply = None
        if has_before:
            before = (ml_in[h : h + 1], ml_in[H + h : H + h + 1], acc_in[c])
        if has_reply:
            reply = (reply_refs[piece][low], totals[piece][inner : inner + 1])
        return q_ref[:, c], given, before, reply

    def store(h, m, l, acc):
        c = slice(h * HD, (h + 1) * HD)
        if last:
            out_hbm, out_ref, sems = refs
            out_ref[:, c] = (acc / l).astype(bf16).T
            if h % 2 == 1:
                n, pair = h // 2, slice((h - 1) * HD, (h + 1) * HD)
                copies.append(
                    pltpu.make_async_copy(out_ref.at[:, pair], out_hbm.at[:, pair], sems.at[n])
                )
                copies[-1].start()
        else:
            refs[0][c] = acc
            tops.append(m)
            sums.append(l)

    over_heads(H, load, store)
    for copy in copies:
        copy.wait()
    if not last:
        refs[1][...] = jnp.concatenate(tops + sums, axis=0)


def local(table, q, sources, before=None, reply=None, last=False):
    vmem = pl.BlockSpec(memory_space=pltpu.VMEM)
    plan = tuple(role for role, _ in sources)
    args = [table, q]
    for role, arrays in sources:
        args += list(arrays) if role == "pairs" else [arrays]
    args += list(before or ()) + list(reply or ())
    if last:
        out_specs = pl.BlockSpec(memory_space=pl.ANY)
        out_shape = jax.ShapeDtypeStruct((ROWS, W), bf16)
        scratch = [pltpu.VMEM((ROWS, W), bf16), pltpu.SemaphoreType.DMA((H // 2,))]
    else:
        scratch = []
        out_specs = [vmem, vmem]
        out_shape = [
            jax.ShapeDtypeStruct((W, ROWS), f32),
            jax.ShapeDtypeStruct((2 * H, ROWS), f32),
        ]
    return pl.pallas_call(
        functools.partial(local_kernel, plan, before is not None, reply is not None, last),
        in_specs=[vmem] * len(args),
        out_specs=out_specs,
        out_shape=out_shape,
        scratch_shapes=scratch,
        compiler_params=pltpu.CompilerParams(vmem_limit_bytes=VMEM_LIMIT),
        cost_estimate=pl.CostEstimate(
            flops=4 * ROWS * ROWS * W, bytes_accessed=1024 * 1024, transcendentals=0
        ),
        name="local_" + "_".join(plan),
    )(*args)


def shards(q, k, v, links, counts):
    ranks = lax.axis_size("rank")
    across = lambda x, to: lax.ppermute(x, "rank", [(i, to(i) % ranks) for i in range(ranks)])
    core = lambda x: across(x, lambda i: i ^ 1)
    to_a = lambda x: lax.ppermute(x, "group", [(i, i ^ 1) for i in range(4)])
    to_b = lambda x: lax.ppermute(x, "group", [(i, 3 - i) for i in range(4)])

    kv, pay_a, pay_b, table = pack(links, counts, q, k, v)
    first = across(kv, lambda i: i + 2 if i % 2 else i - 2)
    from_core = core(kv)
    got_a = [to_a(x) for x in pay_a]
    got_b = [to_b(x) for x in pay_b]
    state = local(table, q, [("own", kv), ("core", from_core)])

    back_a, back_b = [None] * PARTS, [None] * PARTS
    got_a[0], got_b[0], state = lax.optimization_barrier((got_a[0], got_b[0], state))
    kv_later, got_a[0], got_b[0] = lax.optimization_barrier((kv, got_a[0], got_b[0]))
    second = across(kv_later, lambda i: i - 2 if i % 2 else i + 2)
    part_a, part_b = remote(kv, got_a[0], got_b[0], 0)
    back_a[0], back_b[0] = to_a(part_a), to_b(part_b)

    first, part_a = lax.optimization_barrier((first, part_a))
    relay = core(first)
    got_a[1], got_b[1], first = lax.optimization_barrier((got_a[1], got_b[1], first))
    part_a, part_b = remote(kv, got_a[1], got_b[1], 1)
    back_a[1], back_b[1] = to_a(part_a), to_b(part_b)

    state, part_a, back_a[0], back_b[0] = lax.optimization_barrier((state, part_a, back_a[0], back_b[0]))
    state = local(table, q, [("first", first), ("pairs", got_a + got_b)], state)
    second, state = lax.optimization_barrier((second, state))
    return local(table, q, [("second", second), ("relay", relay)], state, back_b + back_a, True)


def solution(mesh):
    rows = P(("group", "rank"), None)
    return jax.shard_map(
        shards,
        mesh=mesh,
        in_specs=(rows, rows, rows, rows, P(("group", "rank"))),
        out_specs=rows,
        check_vma=False,
    )
```

```python
import functools
import math

import jax
import jax.numpy as jnp
from jax import lax
from jax.experimental import pallas as pl
from jax.experimental.pallas import tpu as pltpu
from jax.sharding import PartitionSpec as P

H = 16
HD = 128
LMAX = 8
TILE = 128
ROWS = 256
W = 2048
HALF = W // 2
NEG = -1e30
SCALE = math.log2(math.e) / math.sqrt(HD)
PARTS = 2
PH = H // 2 // PARTS
PW = PH * HD
PAYLOAD = 3 * ROWS + 16
REPLY = PW + 16
SPLIT = 4
VMEM_LIMIT = 20 * 1024 * 1024
REMOTE_COST = (400, 200)

f32 = jnp.float32
bf16 = jnp.bfloat16


def log_multiplicity(links_ref, counts_ref, i, cand, own):
    times = jnp.int32(1 if own else 0)
    for s in range(LMAX):
        hit = (links_ref[i, s] == cand) & (s < counts_ref[i])
        times = times + hit.astype(jnp.int32)
    return jnp.where(times == 0, NEG, jnp.where(times == 1, 0.0, 1.0)).astype(f32)


def score(q, sources):
    raw, tops = [], []
    for k, _, bias in sources:
        s = lax.dot_general(k, q, (((1,), (1,)), ((), ())), preferred_element_type=f32)
        for j in range(2):
            block = s[j * TILE : (j + 1) * TILE]
            raw.append((block, bias[j]))
            tops.append(jnp.max(block, axis=0, keepdims=True) * SCALE + bias[j])
    return raw, tops


def weigh(scored, before=None, reply=None):
    raw, tops = scored
    if before is not None:
        tops = tops + [before[0]]
    if reply is not None:
        tops = tops + [reply[1]]
    m = functools.reduce(jnp.maximum, tops)
    p = [jnp.exp2(block * SCALE + (bias - m)).astype(bf16) for block, bias in raw]
    return m, jnp.concatenate(p, axis=0)


def mix(weighed, sources, before=None, reply=None):
    m, p = weighed
    values = jnp.concatenate([v.T for _, v, _ in sources], axis=1)
    values = jnp.concatenate([values, jnp.ones((16, values.shape[1]), bf16)], axis=0)
    both = jnp.dot(values, p, preferred_element_type=f32)
    acc, l = both[:HD], both[HD : HD + 1]
    if before is not None:
        a = jnp.exp2(before[0] - m)
        acc = acc + before[2] * a
        l = l + before[1] * a
    if reply is not None:
        a = jnp.exp2(reply[1] - m)
        acc = acc + reply[0].astype(f32) * a
        l = l + a
    return m, l, acc


def over_heads(heads, load, store):
    held, scored, weighed = {}, {}, {}
    for t in range(heads + 2):
        if t < heads:
            held[t] = load(t)
            scored[t] = score(*held[t][:2])
        if 0 <= t - 1 < heads:
            weighed[t - 1] = weigh(scored.pop(t - 1), *held[t - 1][2:])
        if t >= 2:
            _, sources, before, reply = held.pop(t - 2)
            store(t - 2, *mix(weighed.pop(t - 2), sources, before, reply))


def payload_heads(way, part):
    return way * HALF + part * PW, (1 - way) * HALF + part * PW


def pack_kernel(links_hbm, counts_hbm, q_hbm, k_hbm, v_hbm, kv_ref, *refs):
    pay_refs, table_ref = refs[: 2 * PARTS], refs[2 * PARTS]
    links_ref, counts_ref, small_sems, sems = refs[2 * PARTS + 1 :]
    small = [
        pltpu.make_async_copy(links_hbm, links_ref, small_sems.at[0]),
        pltpu.make_async_copy(counts_hbm, counts_ref, small_sems.at[1]),
    ]
    for copy in small:
        copy.start()
    copies = []

    def begin(src, dst):
        copies.append(pltpu.make_async_copy(src, dst, sems.at[len(copies)]))
        copies[-1].start()

    step = ROWS // SPLIT
    for n, hbm in enumerate((k_hbm, v_hbm)):
        for i in range(SPLIT):
            begin(hbm.at[pl.ds(i * step, step)], kv_ref.at[pl.ds(n * ROWS + i * step, step)])
    for n, ref in enumerate(pay_refs):
        column = payload_heads(n // PARTS, n % PARTS)[1]
        begin(q_hbm.at[:, pl.ds(column, PW)], ref.at[pl.ds(2 * ROWS, ROWS)])
    for copy in small:
        copy.wait()
    bias = [
        [log_multiplicity(links_ref, counts_ref, i, c, c == i) for i in range(2)]
        for c in range(16)
    ]
    lane = lax.broadcasted_iota(jnp.int32, (16, ROWS), 1)
    row = lax.broadcasted_iota(jnp.int32, (16, ROWS), 0)
    table = jnp.zeros((16, ROWS), f32)
    for c in range(16):
        table = jnp.where(row == c, jnp.where(lane < TILE, bias[c][0], bias[c][1]), table)
    table_ref[...] = table
    even = (lax.axis_index("group") % 2) == 0
    row = lax.broadcasted_iota(jnp.int32, (16, 128), 0)
    for way in range(2):
        extra = jnp.zeros((16, 128), f32)
        for i in range(2):
            for j in range(2):
                one, three = bias[10 + j][i], bias[14 + j][i]
                near = jnp.where(even, one, three) if way == 0 else jnp.where(even, three, one)
                extra = jnp.where(row == 4 * i + j, near, extra)
                extra = jnp.where(row == 4 * i + 2 + j, bias[12 + j][i], extra)
        for ref in pay_refs[way * PARTS : (way + 1) * PARTS]:
            ref[3 * ROWS :, 0:128] = extra.astype(bf16)
            ref[3 * ROWS :, 128:] = jnp.zeros((16, PW - 128), bf16)
    for part in range(2 * SPLIT):
        copies[part].wait()
        rows = slice(part * step, (part + 1) * step)
        for n, ref in enumerate(pay_refs):
            column = payload_heads(n // PARTS, n % PARTS)[0]
            ref[rows] = kv_ref[rows, column : column + PW]
    for copy in copies[2 * SPLIT :]:
        copy.wait()


def pack(links, counts, q, k, v):
    vmem = pl.BlockSpec(memory_space=pltpu.VMEM)
    hbm = pl.BlockSpec(memory_space=pltpu.HBM)
    args = [pltpu.with_memory_space_constraint(x, pltpu.HBM) for x in (links, counts, q, k, v)]
    out = pl.pallas_call(
        pack_kernel,
        in_specs=[hbm] * 5,
        out_specs=[vmem] * (2 + 2 * PARTS),
        out_shape=[jax.ShapeDtypeStruct((2 * ROWS, W), bf16)]
        + [jax.ShapeDtypeStruct((PAYLOAD, PW), bf16)] * (2 * PARTS)
        + [jax.ShapeDtypeStruct((16, ROWS), f32)],
        scratch_shapes=[
            pltpu.SMEM((2, LMAX), jnp.int32),
            pltpu.SMEM((2,), jnp.int32),
            pltpu.SemaphoreType.DMA((2,)),
            pltpu.SemaphoreType.DMA((2 * SPLIT + 2 * PARTS,)),
        ],
        compiler_params=pltpu.CompilerParams(vmem_limit_bytes=VMEM_LIMIT),
        cost_estimate=pl.CostEstimate(flops=0, bytes_accessed=8 * 1024 * 1024, transcendentals=0),
        name="pack",
    )(*args)
    return out[0], out[1 : 1 + PARTS], out[1 + PARTS : 1 + 2 * PARTS], out[-1]


def remote_kernel(part, kv_ref, a_ref, b_ref, out_a, out_b):
    asked, other, outs = (a_ref, b_ref), (b_ref, a_ref), (out_a, out_b)
    bias, stats = [], []
    for way in range(2):
        extra = asked[way][3 * ROWS :, 0:128].astype(f32)
        bias.append(
            [jnp.concatenate([extra[n : n + 1], extra[4 + n : 5 + n]], axis=1) for n in range(4)]
        )
        stats.append([[], [], []])

    def load(h):
        way, inner = h // PH, h % PH
        c = slice(inner * HD, (inner + 1) * HD)
        first = payload_heads(way, part)[1] + inner * HD
        own = slice(first, first + HD)
        sources = [
            (kv_ref[0:ROWS, own], kv_ref[ROWS:, own], bias[way][0:2]),
            (other[way][0:ROWS, c], other[way][ROWS : 2 * ROWS, c], bias[way][2:4]),
        ]
        return asked[way][2 * ROWS : 3 * ROWS, c], sources, None, None

    def store(h, m, l, acc):
        way, inner = h // PH, h % PH
        outs[way][inner * HD : (inner + 1) * HD] = (acc / l).astype(bf16)
        total = m + jnp.log2(l)
        high = total.astype(bf16).astype(f32)
        rest = total - high
        middle = rest.astype(bf16).astype(f32)
        for rows, piece in zip(stats[way], (high, middle, rest - middle)):
            rows.append(piece)

    over_heads(2 * PH, load, store)
    for way in range(2):
        rows = stats[way][0] + stats[way][1] + stats[way][2]
        rows += [jnp.zeros((1, ROWS), f32)] * (16 - len(rows))
        outs[way][PW:] = jnp.concatenate(rows, axis=0).astype(bf16)


def remote(kv, a, b, part):
    vmem = pl.BlockSpec(memory_space=pltpu.VMEM)
    return pl.pallas_call(
        functools.partial(remote_kernel, part),
        in_specs=[vmem] * 3,
        out_specs=[vmem] * 2,
        out_shape=[jax.ShapeDtypeStruct((REPLY, ROWS), bf16)] * 2,
        compiler_params=pltpu.CompilerParams(vmem_limit_bytes=VMEM_LIMIT),
        cost_estimate=pl.CostEstimate(
            flops=REMOTE_COST[part] * ROWS * ROWS * HALF, bytes_accessed=1024 * 1024, transcendentals=0
        ),
        name=f"remote_{part}",
    )(kv, a, b)


def local_kernel(plan, has_before, has_reply, last, *refs):
    refs = list(refs)
    table_ref, q_ref = refs.pop(0), refs.pop(0)
    odd_core = (lax.axis_index("rank") % 2) == 1
    odd_group = (lax.axis_index("group") % 2) == 1
    sources = []
    for role in plan:
        if role == "pairs":
            arrays = [refs.pop(0) for _ in range(2 * PARTS)]
            blocks = (jnp.where(odd_group, 7, 5), jnp.where(odd_group, 5, 7))
        else:
            arrays = refs.pop(0)
            block = {
                "own": 0,
                "core": jnp.where(odd_core, 2, 3),
                "relay": jnp.where(odd_core, 3, 2),
                "first": jnp.where(odd_core, 1, 4),
                "second": jnp.where(odd_core, 4, 1),
            }[role]
            blocks = (block, block)
        bias = [
            [table_ref[pl.ds(block * 2 + j, 1), :] for j in range(2)] for block in blocks
        ]
        sources.append((role, arrays, bias))
    if has_before:
        acc_in, ml_in = refs.pop(0), refs.pop(0)
    if has_reply:
        reply_refs = [refs.pop(0) for _ in range(2 * PARTS)]
        totals = []
        for ref in reply_refs:
            tail = ref[PW:].astype(f32)
            totals.append(tail[0:PH] + tail[PH : 2 * PH] + tail[2 * PH : 3 * PH])
    tops, sums, copies = [], [], []

    def load(h):
        piece, inner = h // PH, h % PH
        half = h // (H // 2)
        c = slice(h * HD, (h + 1) * HD)
        low = slice(inner * HD, (inner + 1) * HD)
        given = []
        for role, arrays, bias in sources:
            array, at = (arrays[piece], low) if role == "pairs" else (arrays, c)
            given.append((array[0:ROWS, at], array[ROWS : 2 * ROWS, at], bias[half]))
        before = reply = None
        if has_before:
            before = (ml_in[h : h + 1], ml_in[H + h : H + h + 1], acc_in[c])
        if has_reply:
            reply = (reply_refs[piece][low], totals[piece][inner : inner + 1])
        return q_ref[:, c], given, before, reply

    def store(h, m, l, acc):
        c = slice(h * HD, (h + 1) * HD)
        if last:
            out_hbm, out_ref, sems = refs
            out_ref[:, c] = (acc / l).astype(bf16).T
            if h % 2 == 1:
                n, pair = h // 2, slice((h - 1) * HD, (h + 1) * HD)
                copies.append(
                    pltpu.make_async_copy(out_ref.at[:, pair], out_hbm.at[:, pair], sems.at[n])
                )
                copies[-1].start()
        else:
            refs[0][c] = acc
            tops.append(m)
            sums.append(l)

    over_heads(H, load, store)
    for copy in copies:
        copy.wait()
    if not last:
        refs[1][...] = jnp.concatenate(tops + sums, axis=0)


def local(table, q, sources, before=None, reply=None, last=False):
    vmem = pl.BlockSpec(memory_space=pltpu.VMEM)
    plan = tuple(role for role, _ in sources)
    args = [table, q]
    for role, arrays in sources:
        args += list(arrays) if role == "pairs" else [arrays]
    args += list(before or ()) + list(reply or ())
    if last:
        out_specs = pl.BlockSpec(memory_space=pl.ANY)
        out_shape = jax.ShapeDtypeStruct((ROWS, W), bf16)
        scratch = [pltpu.VMEM((ROWS, W), bf16), pltpu.SemaphoreType.DMA((H // 2,))]
    else:
        scratch = []
        out_specs = [vmem, vmem]
        out_shape = [
            jax.ShapeDtypeStruct((W, ROWS), f32),
            jax.ShapeDtypeStruct((2 * H, ROWS), f32),
        ]
    return pl.pallas_call(
        functools.partial(local_kernel, plan, before is not None, reply is not None, last),
        in_specs=[vmem] * len(args),
        out_specs=out_specs,
        out_shape=out_shape,
        scratch_shapes=scratch,
        compiler_params=pltpu.CompilerParams(vmem_limit_bytes=VMEM_LIMIT),
        cost_estimate=pl.CostEstimate(
            flops=4 * ROWS * ROWS * W, bytes_accessed=1024 * 1024, transcendentals=0
        ),
        name="local_" + "_".join(plan),
    )(*args)


def shards(q, k, v, links, counts):
    ranks = lax.axis_size("rank")
    across = lambda x, to: lax.ppermute(x, "rank", [(i, to(i) % ranks) for i in range(ranks)])
    core = lambda x: across(x, lambda i: i ^ 1)
    to_a = lambda x: lax.ppermute(x, "group", [(i, i ^ 1) for i in range(4)])
    to_b = lambda x: lax.ppermute(x, "group", [(i, 3 - i) for i in range(4)])

    kv, pay_a, pay_b, table = pack(links, counts, q, k, v)
    first = across(kv, lambda i: i + 2 if i % 2 else i - 2)
    from_core = core(kv)
    got_a = [to_a(x) for x in pay_a]
    got_b = [to_b(x) for x in pay_b]
    state = local(table, q, [("own", kv), ("core", from_core)])

    back_a, back_b = [None] * PARTS, [None] * PARTS
    got_a[0], got_b[0], state = lax.optimization_barrier((got_a[0], got_b[0], state))
    kv_later, got_a[0], got_b[0] = lax.optimization_barrier((kv, got_a[0], got_b[0]))
    second = across(kv_later, lambda i: i - 2 if i % 2 else i + 2)
    part_a, part_b = remote(kv, got_a[0], got_b[0], 0)
    back_a[0], back_b[0] = to_a(part_a), to_b(part_b)

    first, part_a = lax.optimization_barrier((first, part_a))
    relay = core(first)
    got_a[1], got_b[1], first = lax.optimization_barrier((got_a[1], got_b[1], first))
    part_a, part_b = remote(kv, got_a[1], got_b[1], 1)
    part_a, back_a[0] = lax.optimization_barrier((part_a, back_a[0]))
    back_a[1], back_b[1] = to_a(part_a), to_b(part_b)

    state, part_a, back_a[0], back_b[0] = lax.optimization_barrier((state, part_a, back_a[0], back_b[0]))
    state = local(table, q, [("first", first), ("pairs", got_a + got_b)], state)
    second, state = lax.optimization_barrier((second, state))
    return local(table, q, [("second", second), ("relay", relay)], state, back_b + back_a, True)


def solution(mesh):
    rows = P(("group", "rank"), None)
    return jax.shard_map(
        shards,
        mesh=mesh,
        in_specs=(rows, rows, rows, rows, P(("group", "rank"))),
        out_specs=rows,
        check_vma=False,
    )
```

```python
import functools
import math

import jax
import jax.numpy as jnp
from jax import lax
from jax.experimental import pallas as pl
from jax.experimental.pallas import tpu as pltpu
from jax.sharding import PartitionSpec as P

H = 16
HD = 128
LMAX = 8
TILE = 128
ROWS = 256
W = 2048
HALF = W // 2
NEG = -1e30
SCALE = math.log2(math.e) / math.sqrt(HD)
PARTS = 2
PH = H // 2 // PARTS
PW = PH * HD
PAYLOAD = 3 * ROWS + 16
REPLY = PW + 16
SPLIT = 4
VMEM_LIMIT = 20 * 1024 * 1024
REMOTE_COST = (400, 8)
MIDDLE_COST = 22

f32 = jnp.float32
bf16 = jnp.bfloat16


def log_multiplicity(links_ref, counts_ref, i, cand, own):
    times = jnp.int32(1 if own else 0)
    for s in range(LMAX):
        hit = (links_ref[i, s] == cand) & (s < counts_ref[i])
        times = times + hit.astype(jnp.int32)
    return jnp.where(times == 0, NEG, jnp.where(times == 1, 0.0, 1.0)).astype(f32)


def score(q, sources):
    raw, tops = [], []
    for k, _, bias in sources:
        s = lax.dot_general(k, q, (((1,), (1,)), ((), ())), preferred_element_type=f32)
        for j in range(2):
            block = s[j * TILE : (j + 1) * TILE]
            raw.append((block, bias[j]))
            tops.append(jnp.max(block, axis=0, keepdims=True) * SCALE + bias[j])
    return raw, tops


def weigh(scored, before=None, reply=None):
    raw, tops = scored
    if before is not None:
        tops = tops + [before[0]]
    if reply is not None:
        tops = tops + [reply[1]]
    m = functools.reduce(jnp.maximum, tops)
    p = [jnp.exp2(block * SCALE + (bias - m)).astype(bf16) for block, bias in raw]
    return m, jnp.concatenate(p, axis=0)


def mix(weighed, sources, before=None, reply=None):
    m, p = weighed
    values = jnp.concatenate([v.T for _, v, _ in sources], axis=1)
    values = jnp.concatenate([values, jnp.ones((16, values.shape[1]), bf16)], axis=0)
    both = jnp.dot(values, p, preferred_element_type=f32)
    acc, l = both[:HD], both[HD : HD + 1]
    if before is not None:
        a = jnp.exp2(before[0] - m)
        acc = acc + before[2] * a
        l = l + before[1] * a
    if reply is not None:
        a = jnp.exp2(reply[1] - m)
        acc = acc + reply[0].astype(f32) * a
        l = l + a
    return m, l, acc


def over_heads(heads, load, store):
    held, scored, weighed = {}, {}, {}
    for t in range(heads + 2):
        if t < heads:
            held[t] = load(t)
            scored[t] = score(*held[t][:2])
        if 0 <= t - 1 < heads:
            weighed[t - 1] = weigh(scored.pop(t - 1), *held[t - 1][2:])
        if t >= 2:
            _, sources, before, reply = held.pop(t - 2)
            store(t - 2, *mix(weighed.pop(t - 2), sources, before, reply))


def payload_heads(way, part):
    return way * HALF + part * PW, (1 - way) * HALF + part * PW


def pack_kernel(links_hbm, counts_hbm, q_hbm, k_hbm, v_hbm, kv_ref, *refs):
    pay_refs, table_ref = refs[: 2 * PARTS], refs[2 * PARTS]
    links_ref, counts_ref, small_sems, sems = refs[2 * PARTS + 1 :]
    small = [
        pltpu.make_async_copy(links_hbm, links_ref, small_sems.at[0]),
        pltpu.make_async_copy(counts_hbm, counts_ref, small_sems.at[1]),
    ]
    for copy in small:
        copy.start()
    copies = []

    def begin(src, dst):
        copies.append(pltpu.make_async_copy(src, dst, sems.at[len(copies)]))
        copies[-1].start()

    step = ROWS // SPLIT
    for n, hbm in enumerate((k_hbm, v_hbm)):
        for i in range(SPLIT):
            begin(hbm.at[pl.ds(i * step, step)], kv_ref.at[pl.ds(n * ROWS + i * step, step)])
    for n, ref in enumerate(pay_refs):
        column = payload_heads(n // PARTS, n % PARTS)[1]
        begin(q_hbm.at[:, pl.ds(column, PW)], ref.at[pl.ds(2 * ROWS, ROWS)])
    for copy in small:
        copy.wait()
    bias = [
        [log_multiplicity(links_ref, counts_ref, i, c, c == i) for i in range(2)]
        for c in range(16)
    ]
    lane = lax.broadcasted_iota(jnp.int32, (16, ROWS), 1)
    row = lax.broadcasted_iota(jnp.int32, (16, ROWS), 0)
    table = jnp.zeros((16, ROWS), f32)
    for c in range(16):
        table = jnp.where(row == c, jnp.where(lane < TILE, bias[c][0], bias[c][1]), table)
    table_ref[...] = table
    even = (lax.axis_index("group") % 2) == 0
    row = lax.broadcasted_iota(jnp.int32, (16, 128), 0)
    for way in range(2):
        extra = jnp.zeros((16, 128), f32)
        for i in range(2):
            for j in range(2):
                one, three = bias[10 + j][i], bias[14 + j][i]
                near = jnp.where(even, one, three) if way == 0 else jnp.where(even, three, one)
                extra = jnp.where(row == 4 * i + j, near, extra)
                extra = jnp.where(row == 4 * i + 2 + j, bias[12 + j][i], extra)
        for ref in pay_refs[way * PARTS : (way + 1) * PARTS]:
            ref[3 * ROWS :, 0:128] = extra.astype(bf16)
            ref[3 * ROWS :, 128:] = jnp.zeros((16, PW - 128), bf16)
    for part in range(2 * SPLIT):
        copies[part].wait()
        rows = slice(part * step, (part + 1) * step)
        for n, ref in enumerate(pay_refs):
            column = payload_heads(n // PARTS, n % PARTS)[0]
            ref[rows] = kv_ref[rows, column : column + PW]
    for copy in copies[2 * SPLIT :]:
        copy.wait()


def pack(links, counts, q, k, v):
    vmem = pl.BlockSpec(memory_space=pltpu.VMEM)
    hbm = pl.BlockSpec(memory_space=pltpu.HBM)
    args = [pltpu.with_memory_space_constraint(x, pltpu.HBM) for x in (links, counts, q, k, v)]
    out = pl.pallas_call(
        pack_kernel,
        in_specs=[hbm] * 5,
        out_specs=[vmem] * (2 + 2 * PARTS),
        out_shape=[jax.ShapeDtypeStruct((2 * ROWS, W), bf16)]
        + [jax.ShapeDtypeStruct((PAYLOAD, PW), bf16)] * (2 * PARTS)
        + [jax.ShapeDtypeStruct((16, ROWS), f32)],
        scratch_shapes=[
            pltpu.SMEM((2, LMAX), jnp.int32),
            pltpu.SMEM((2,), jnp.int32),
            pltpu.SemaphoreType.DMA((2,)),
            pltpu.SemaphoreType.DMA((2 * SPLIT + 2 * PARTS,)),
        ],
        compiler_params=pltpu.CompilerParams(vmem_limit_bytes=VMEM_LIMIT),
        cost_estimate=pl.CostEstimate(flops=0, bytes_accessed=8 * 1024 * 1024, transcendentals=0),
        name="pack",
    )(*args)
    return out[0], out[1 : 1 + PARTS], out[1 + PARTS : 1 + 2 * PARTS], out[-1]


def remote_kernel(part, kv_ref, a_ref, b_ref, out_a, out_b):
    asked, other, outs = (a_ref, b_ref), (b_ref, a_ref), (out_a, out_b)
    bias, stats = [], []
    for way in range(2):
        extra = asked[way][3 * ROWS :, 0:128].astype(f32)
        bias.append(
            [jnp.concatenate([extra[n : n + 1], extra[4 + n : 5 + n]], axis=1) for n in range(4)]
        )
        stats.append([[], [], []])

    def load(h):
        way, inner = h // PH, h % PH
        c = slice(inner * HD, (inner + 1) * HD)
        first = payload_heads(way, part)[1] + inner * HD
        own = slice(first, first + HD)
        sources = [
            (kv_ref[0:ROWS, own], kv_ref[ROWS:, own], bias[way][0:2]),
            (other[way][0:ROWS, c], other[way][ROWS : 2 * ROWS, c], bias[way][2:4]),
        ]
        return asked[way][2 * ROWS : 3 * ROWS, c], sources, None, None

    def store(h, m, l, acc):
        way, inner = h // PH, h % PH
        outs[way][inner * HD : (inner + 1) * HD] = (acc / l).astype(bf16)
        total = m + jnp.log2(l)
        high = total.astype(bf16).astype(f32)
        rest = total - high
        middle = rest.astype(bf16).astype(f32)
        for rows, piece in zip(stats[way], (high, middle, rest - middle)):
            rows.append(piece)

    over_heads(2 * PH, load, store)
    for way in range(2):
        rows = stats[way][0] + stats[way][1] + stats[way][2]
        rows += [jnp.zeros((1, ROWS), f32)] * (16 - len(rows))
        outs[way][PW:] = jnp.concatenate(rows, axis=0).astype(bf16)


def remote(kv, a, b, part):
    vmem = pl.BlockSpec(memory_space=pltpu.VMEM)
    return pl.pallas_call(
        functools.partial(remote_kernel, part),
        in_specs=[vmem] * 3,
        out_specs=[vmem] * 2,
        out_shape=[jax.ShapeDtypeStruct((REPLY, ROWS), bf16)] * 2,
        compiler_params=pltpu.CompilerParams(vmem_limit_bytes=VMEM_LIMIT),
        cost_estimate=pl.CostEstimate(
            flops=REMOTE_COST[part] * ROWS * ROWS * HALF, bytes_accessed=1024 * 1024, transcendentals=0
        ),
        name=f"remote_{part}",
    )(kv, a, b)


def local_kernel(plan, has_before, has_reply, last, *refs):
    refs = list(refs)
    table_ref, q_ref = refs.pop(0), refs.pop(0)
    odd_core = (lax.axis_index("rank") % 2) == 1
    odd_group = (lax.axis_index("group") % 2) == 1
    sources = []
    for role in plan:
        if role == "relay":
            arrays = [refs.pop(0), refs.pop(0)]
            block = jnp.where(odd_core, 3, 2)
            blocks = (block, block)
        elif role == "pairs":
            arrays = [refs.pop(0) for _ in range(2 * PARTS)]
            blocks = (jnp.where(odd_group, 7, 5), jnp.where(odd_group, 5, 7))
        else:
            arrays = refs.pop(0)
            block = {
                "own": 0,
                "core": jnp.where(odd_core, 2, 3),
                "first": jnp.where(odd_core, 1, 4),
                "second": jnp.where(odd_core, 4, 1),
            }[role]
            blocks = (block, block)
        bias = [
            [table_ref[pl.ds(block * 2 + j, 1), :] for j in range(2)] for block in blocks
        ]
        sources.append((role, arrays, bias))
    if has_before:
        acc_in, ml_in = refs.pop(0), refs.pop(0)
    if has_reply:
        reply_refs = [refs.pop(0) for _ in range(2 * PARTS)]
        totals = []
        for ref in reply_refs:
            tail = ref[PW:].astype(f32)
            totals.append(tail[0:PH] + tail[PH : 2 * PH] + tail[2 * PH : 3 * PH])
    tops, sums, copies = [], [], []

    def load(h):
        piece, inner = h // PH, h % PH
        half = h // (H // 2)
        c = slice(h * HD, (h + 1) * HD)
        low = slice(inner * HD, (inner + 1) * HD)
        given = []
        for role, arrays, bias in sources:
            if role == "relay":
                given.append((arrays[0][:, c], arrays[1][:, c], bias[half]))
                continue
            array, at = (arrays[piece], low) if role == "pairs" else (arrays, c)
            given.append((array[0:ROWS, at], array[ROWS : 2 * ROWS, at], bias[half]))
        before = reply = None
        if has_before:
            before = (ml_in[h : h + 1], ml_in[H + h : H + h + 1], acc_in[c])
        if has_reply:
            reply = (reply_refs[piece][low], totals[piece][inner : inner + 1])
        return q_ref[:, c], given, before, reply

    def store(h, m, l, acc):
        c = slice(h * HD, (h + 1) * HD)
        if last:
            out_hbm, out_ref, sems = refs
            out_ref[:, c] = (acc / l).astype(bf16).T
            if h % 2 == 1:
                n, pair = h // 2, slice((h - 1) * HD, (h + 1) * HD)
                copies.append(
                    pltpu.make_async_copy(out_ref.at[:, pair], out_hbm.at[:, pair], sems.at[n])
                )
                copies[-1].start()
        else:
            refs[0][c] = acc
            tops.append(m)
            sums.append(l)

    over_heads(H, load, store)
    for copy in copies:
        copy.wait()
    if not last:
        refs[1][...] = jnp.concatenate(tops + sums, axis=0)


def local(table, q, sources, before=None, reply=None, last=False, cost=1):
    vmem = pl.BlockSpec(memory_space=pltpu.VMEM)
    plan = tuple(role for role, _ in sources)
    args = [table, q]
    for role, arrays in sources:
        args += list(arrays) if role in ("pairs", "relay") else [arrays]
    args += list(before or ()) + list(reply or ())
    if last:
        out_specs = pl.BlockSpec(memory_space=pl.ANY)
        out_shape = jax.ShapeDtypeStruct((ROWS, W), bf16)
        scratch = [pltpu.VMEM((ROWS, W), bf16), pltpu.SemaphoreType.DMA((H // 2,))]
    else:
        scratch = []
        out_specs = [vmem, vmem]
        out_shape = [
            jax.ShapeDtypeStruct((W, ROWS), f32),
            jax.ShapeDtypeStruct((2 * H, ROWS), f32),
        ]
    return pl.pallas_call(
        functools.partial(local_kernel, plan, before is not None, reply is not None, last),
        in_specs=[vmem] * len(args),
        out_specs=out_specs,
        out_shape=out_shape,
        scratch_shapes=scratch,
        compiler_params=pltpu.CompilerParams(vmem_limit_bytes=VMEM_LIMIT),
        cost_estimate=pl.CostEstimate(
            flops=4 * cost * ROWS * ROWS * W, bytes_accessed=1024 * 1024, transcendentals=0
        ),
        name="local_" + "_".join(plan),
    )(*args)


def shards(q, k, v, links, counts):
    ranks = lax.axis_size("rank")
    across = lambda x, to: lax.ppermute(x, "rank", [(i, to(i) % ranks) for i in range(ranks)])
    core = lambda x: across(x, lambda i: i ^ 1)
    to_a = lambda x: lax.ppermute(x, "group", [(i, i ^ 1) for i in range(4)])
    to_b = lambda x: lax.ppermute(x, "group", [(i, 3 - i) for i in range(4)])

    kv, pay_a, pay_b, table = pack(links, counts, q, k, v)
    first = across(kv, lambda i: i + 2 if i % 2 else i - 2)
    from_core = core(kv)
    got_a = [to_a(pay_a[0]), to_a(pay_a[1])]
    got_b = [to_b(pay_b[0])]
    kv_later, from_core = lax.optimization_barrier((kv, from_core))
    second = across(kv_later, lambda i: i - 2 if i % 2 else i + 2)
    state = local(table, q, [("own", kv), ("core", from_core)])

    back_a, back_b = [None] * PARTS, [None] * PARTS
    got_a[0], got_b[0], state = lax.optimization_barrier((got_a[0], got_b[0], state))
    pay, got_a[0] = lax.optimization_barrier((pay_b[1], got_a[0]))
    got_b.append(to_b(pay))
    part_a, part_b = remote(kv, got_a[0], got_b[0], 0)
    back_a[0], back_b[0] = to_a(part_a), to_b(part_b)

    got_a[1], got_b[1], part_a = lax.optimization_barrier((got_a[1], got_b[1], part_a))
    part_a, part_b = remote(kv, got_a[1], got_b[1], 1)
    part_a, back_a[0] = lax.optimization_barrier((part_a, back_a[0]))
    part_b, back_b[0] = lax.optimization_barrier((part_b, back_b[0]))
    back_a[1], back_b[1] = to_a(part_a), to_b(part_b)

    first, part_a, part_b = lax.optimization_barrier((first, part_a, part_b))
    relay = [core(first[:ROWS]), core(first[ROWS:])]
    state, part_a = lax.optimization_barrier((state, part_a))
    middle = [("first", first), ("pairs", got_a + got_b)]
    state = local(table, q, middle, state, cost=MIDDLE_COST)
    second, state = lax.optimization_barrier((second, state))
    near = [("second", second), ("relay", relay)]
    return local(table, q, near, state, back_b + back_a, True)


def solution(mesh):
    rows = P(("group", "rank"), None)
    return jax.shard_map(
        shards,
        mesh=mesh,
        in_specs=(rows, rows, rows, rows, P(("group", "rank"))),
        out_specs=rows,
        check_vma=False,
    )
```

```python
import functools
import math

import jax
import jax.numpy as jnp
from jax import lax
from jax.experimental import pallas as pl
from jax.experimental.pallas import tpu as pltpu
from jax.sharding import PartitionSpec as P

H = 16
HD = 128
LMAX = 8
TILE = 128
ROWS = 256
W = 2048
HALF = W // 2
NEG = -1e30
SCALE = math.log2(math.e) / math.sqrt(HD)
PARTS = 2
PH = H // 2 // PARTS
PW = PH * HD
PAYLOAD = 3 * ROWS + 16
REPLY = PW + 16
SPLIT = 4
VMEM_LIMIT = 20 * 1024 * 1024
REMOTE_COST = (400, 200)
MIDDLE_COST = 1

f32 = jnp.float32
bf16 = jnp.bfloat16


def log_multiplicity(links_ref, counts_ref, i, cand, own):
    times = jnp.int32(1 if own else 0)
    for s in range(LMAX):
        hit = (links_ref[i, s] == cand) & (s < counts_ref[i])
        times = times + hit.astype(jnp.int32)
    return jnp.where(times == 0, NEG, jnp.where(times == 1, 0.0, 1.0)).astype(f32)


def score(q, sources):
    raw, tops = [], []
    for k, _, bias in sources:
        s = lax.dot_general(k, q, (((1,), (1,)), ((), ())), preferred_element_type=f32)
        for j in range(2):
            block = s[j * TILE : (j + 1) * TILE]
            raw.append((block, bias[j]))
            tops.append(jnp.max(block, axis=0, keepdims=True) * SCALE + bias[j])
    return raw, tops


def weigh(scored, before=None, reply=None):
    raw, tops = scored
    if before is not None:
        tops = tops + [before[0]]
    if reply is not None:
        tops = tops + [reply[1]]
    m = functools.reduce(jnp.maximum, tops)
    p = [jnp.exp2(block * SCALE + (bias - m)).astype(bf16) for block, bias in raw]
    return m, jnp.concatenate(p, axis=0)


def mix(weighed, sources, before=None, reply=None):
    m, p = weighed
    values = jnp.concatenate([v.T for _, v, _ in sources], axis=1)
    values = jnp.concatenate([values, jnp.ones((16, values.shape[1]), bf16)], axis=0)
    both = jnp.dot(values, p, preferred_element_type=f32)
    acc, l = both[:HD], both[HD : HD + 1]
    if before is not None:
        a = jnp.exp2(before[0] - m)
        acc = acc + before[2] * a
        l = l + before[1] * a
    if reply is not None:
        a = jnp.exp2(reply[1] - m)
        acc = acc + reply[0].astype(f32) * a
        l = l + a
    return m, l, acc


def over_heads(heads, load, store):
    held, scored, weighed = {}, {}, {}
    for t in range(heads + 2):
        if t < heads:
            held[t] = load(t)
            scored[t] = score(*held[t][:2])
        if 0 <= t - 1 < heads:
            weighed[t - 1] = weigh(scored.pop(t - 1), *held[t - 1][2:])
        if t >= 2:
            _, sources, before, reply = held.pop(t - 2)
            store(t - 2, *mix(weighed.pop(t - 2), sources, before, reply))


def payload_heads(way, part):
    return way * HALF + part * PW, (1 - way) * HALF + part * PW


def pack_kernel(links_hbm, counts_hbm, q_hbm, k_hbm, v_hbm, kv_ref, *refs):
    pay_refs, table_ref = refs[: 2 * PARTS], refs[2 * PARTS]
    links_ref, counts_ref, small_sems, sems = refs[2 * PARTS + 1 :]
    small = [
        pltpu.make_async_copy(links_hbm, links_ref, small_sems.at[0]),
        pltpu.make_async_copy(counts_hbm, counts_ref, small_sems.at[1]),
    ]
    for copy in small:
        copy.start()
    copies = []

    def begin(src, dst):
        copies.append(pltpu.make_async_copy(src, dst, sems.at[len(copies)]))
        copies[-1].start()

    step = ROWS // SPLIT
    for n, hbm in enumerate((k_hbm, v_hbm)):
        for i in range(SPLIT):
            begin(hbm.at[pl.ds(i * step, step)], kv_ref.at[pl.ds(n * ROWS + i * step, step)])
    for n, ref in enumerate(pay_refs):
        column = payload_heads(n // PARTS, n % PARTS)[1]
        begin(q_hbm.at[:, pl.ds(column, PW)], ref.at[pl.ds(2 * ROWS, ROWS)])
    for copy in small:
        copy.wait()
    bias = [
        [log_multiplicity(links_ref, counts_ref, i, c, c == i) for i in range(2)]
        for c in range(16)
    ]
    lane = lax.broadcasted_iota(jnp.int32, (16, ROWS), 1)
    row = lax.broadcasted_iota(jnp.int32, (16, ROWS), 0)
    table = jnp.zeros((16, ROWS), f32)
    for c in range(16):
        table = jnp.where(row == c, jnp.where(lane < TILE, bias[c][0], bias[c][1]), table)
    table_ref[...] = table
    even = (lax.axis_index("group") % 2) == 0
    row = lax.broadcasted_iota(jnp.int32, (16, 128), 0)
    for way in range(2):
        extra = jnp.zeros((16, 128), f32)
        for i in range(2):
            for j in range(2):
                one, three = bias[10 + j][i], bias[14 + j][i]
                near = jnp.where(even, one, three) if way == 0 else jnp.where(even, three, one)
                extra = jnp.where(row == 4 * i + j, near, extra)
                extra = jnp.where(row == 4 * i + 2 + j, bias[12 + j][i], extra)
        for ref in pay_refs[way * PARTS : (way + 1) * PARTS]:
            ref[3 * ROWS :, 0:128] = extra.astype(bf16)
            ref[3 * ROWS :, 128:] = jnp.zeros((16, PW - 128), bf16)
    for part in range(2 * SPLIT):
        copies[part].wait()
        rows = slice(part * step, (part + 1) * step)
        for n, ref in enumerate(pay_refs):
            column = payload_heads(n // PARTS, n % PARTS)[0]
            ref[rows] = kv_ref[rows, column : column + PW]
    for copy in copies[2 * SPLIT :]:
        copy.wait()


def pack(links, counts, q, k, v):
    vmem = pl.BlockSpec(memory_space=pltpu.VMEM)
    hbm = pl.BlockSpec(memory_space=pltpu.HBM)
    args = [pltpu.with_memory_space_constraint(x, pltpu.HBM) for x in (links, counts, q, k, v)]
    out = pl.pallas_call(
        pack_kernel,
        in_specs=[hbm] * 5,
        out_specs=[vmem] * (2 + 2 * PARTS),
        out_shape=[jax.ShapeDtypeStruct((2 * ROWS, W), bf16)]
        + [jax.ShapeDtypeStruct((PAYLOAD, PW), bf16)] * (2 * PARTS)
        + [jax.ShapeDtypeStruct((16, ROWS), f32)],
        scratch_shapes=[
            pltpu.SMEM((2, LMAX), jnp.int32),
            pltpu.SMEM((2,), jnp.int32),
            pltpu.SemaphoreType.DMA((2,)),
            pltpu.SemaphoreType.DMA((2 * SPLIT + 2 * PARTS,)),
        ],
        compiler_params=pltpu.CompilerParams(vmem_limit_bytes=VMEM_LIMIT),
        cost_estimate=pl.CostEstimate(flops=0, bytes_accessed=8 * 1024 * 1024, transcendentals=0),
        name="pack",
    )(*args)
    return out[0], out[1 : 1 + PARTS], out[1 + PARTS : 1 + 2 * PARTS], out[-1]


def remote_kernel(part, kv_ref, a_ref, b_ref, out_a, out_b):
    asked, other, outs = (a_ref, b_ref), (b_ref, a_ref), (out_a, out_b)
    bias, stats = [], []
    for way in range(2):
        extra = asked[way][3 * ROWS :, 0:128].astype(f32)
        bias.append(
            [jnp.concatenate([extra[n : n + 1], extra[4 + n : 5 + n]], axis=1) for n in range(4)]
        )
        stats.append([[], [], []])

    def load(h):
        way, inner = h // PH, h % PH
        c = slice(inner * HD, (inner + 1) * HD)
        first = payload_heads(way, part)[1] + inner * HD
        own = slice(first, first + HD)
        sources = [
            (kv_ref[0:ROWS, own], kv_ref[ROWS:, own], bias[way][0:2]),
            (other[way][0:ROWS, c], other[way][ROWS : 2 * ROWS, c], bias[way][2:4]),
        ]
        return asked[way][2 * ROWS : 3 * ROWS, c], sources, None, None

    def store(h, m, l, acc):
        way, inner = h // PH, h % PH
        outs[way][inner * HD : (inner + 1) * HD] = (acc / l).astype(bf16)
        total = m + jnp.log2(l)
        high = total.astype(bf16).astype(f32)
        rest = total - high
        middle = rest.astype(bf16).astype(f32)
        for rows, piece in zip(stats[way], (high, middle, rest - middle)):
            rows.append(piece)

    over_heads(2 * PH, load, store)
    for way in range(2):
        rows = stats[way][0] + stats[way][1] + stats[way][2]
        rows += [jnp.zeros((1, ROWS), f32)] * (16 - len(rows))
        outs[way][PW:] = jnp.concatenate(rows, axis=0).astype(bf16)


def remote(kv, a, b, part):
    vmem = pl.BlockSpec(memory_space=pltpu.VMEM)
    return pl.pallas_call(
        functools.partial(remote_kernel, part),
        in_specs=[vmem] * 3,
        out_specs=[vmem] * 2,
        out_shape=[jax.ShapeDtypeStruct((REPLY, ROWS), bf16)] * 2,
        compiler_params=pltpu.CompilerParams(vmem_limit_bytes=VMEM_LIMIT),
        cost_estimate=pl.CostEstimate(
            flops=REMOTE_COST[part] * ROWS * ROWS * HALF, bytes_accessed=1024 * 1024, transcendentals=0
        ),
        name=f"remote_{part}",
    )(kv, a, b)


def local_kernel(plan, has_before, has_reply, last, *refs):
    refs = list(refs)
    table_ref, q_ref = refs.pop(0), refs.pop(0)
    odd_core = (lax.axis_index("rank") % 2) == 1
    odd_group = (lax.axis_index("group") % 2) == 1
    sources = []
    for role in plan:
        if role == "relay":
            arrays = [refs.pop(0), refs.pop(0)]
            block = jnp.where(odd_core, 3, 2)
            blocks = (block, block)
        elif role == "pairs":
            arrays = [refs.pop(0) for _ in range(2 * PARTS)]
            blocks = (jnp.where(odd_group, 7, 5), jnp.where(odd_group, 5, 7))
        else:
            arrays = refs.pop(0)
            block = {
                "own": 0,
                "core": jnp.where(odd_core, 2, 3),
                "first": jnp.where(odd_core, 1, 4),
                "second": jnp.where(odd_core, 4, 1),
            }[role]
            blocks = (block, block)
        bias = [
            [table_ref[pl.ds(block * 2 + j, 1), :] for j in range(2)] for block in blocks
        ]
        sources.append((role, arrays, bias))
    if has_before:
        acc_in, ml_in = refs.pop(0), refs.pop(0)
    if has_reply:
        reply_refs = [refs.pop(0) for _ in range(2 * PARTS)]
        totals = []
        for ref in reply_refs:
            tail = ref[PW:].astype(f32)
            totals.append(tail[0:PH] + tail[PH : 2 * PH] + tail[2 * PH : 3 * PH])
    tops, sums, copies = [], [], []

    def load(h):
        piece, inner = h // PH, h % PH
        half = h // (H // 2)
        c = slice(h * HD, (h + 1) * HD)
        low = slice(inner * HD, (inner + 1) * HD)
        given = []
        for role, arrays, bias in sources:
            if role == "relay":
                given.append((arrays[0][:, c], arrays[1][:, c], bias[half]))
                continue
            array, at = (arrays[piece], low) if role == "pairs" else (arrays, c)
            given.append((array[0:ROWS, at], array[ROWS : 2 * ROWS, at], bias[half]))
        before = reply = None
        if has_before:
            before = (ml_in[h : h + 1], ml_in[H + h : H + h + 1], acc_in[c])
        if has_reply:
            reply = (reply_refs[piece][low], totals[piece][inner : inner + 1])
        return q_ref[:, c], given, before, reply

    def store(h, m, l, acc):
        c = slice(h * HD, (h + 1) * HD)
        if last:
            out_hbm, out_ref, sems = refs
            out_ref[:, c] = (acc / l).astype(bf16).T
            copies.append(pltpu.make_async_copy(out_ref.at[:, c], out_hbm.at[:, c], sems.at[h]))
            copies[-1].start()
        else:
            refs[0][c] = acc
            tops.append(m)
            sums.append(l)

    over_heads(H, load, store)
    for copy in copies:
        copy.wait()
    if not last:
        refs[1][...] = jnp.concatenate(tops + sums, axis=0)


def local(table, q, sources, before=None, reply=None, last=False, cost=1):
    vmem = pl.BlockSpec(memory_space=pltpu.VMEM)
    plan = tuple(role for role, _ in sources)
    args = [table, q]
    for role, arrays in sources:
        args += list(arrays) if role in ("pairs", "relay") else [arrays]
    args += list(before or ()) + list(reply or ())
    if last:
        out_specs = pl.BlockSpec(memory_space=pl.ANY)
        out_shape = jax.ShapeDtypeStruct((ROWS, W), bf16)
        scratch = [pltpu.VMEM((ROWS, W), bf16), pltpu.SemaphoreType.DMA((H,))]
    else:
        scratch = []
        out_specs = [vmem, vmem]
        out_shape = [
            jax.ShapeDtypeStruct((W, ROWS), f32),
            jax.ShapeDtypeStruct((2 * H, ROWS), f32),
        ]
    return pl.pallas_call(
        functools.partial(local_kernel, plan, before is not None, reply is not None, last),
        in_specs=[vmem] * len(args),
        out_specs=out_specs,
        out_shape=out_shape,
        scratch_shapes=scratch,
        compiler_params=pltpu.CompilerParams(vmem_limit_bytes=VMEM_LIMIT),
        cost_estimate=pl.CostEstimate(
            flops=4 * cost * ROWS * ROWS * W, bytes_accessed=1024 * 1024, transcendentals=0
        ),
        name="local_" + "_".join(plan),
    )(*args)


def shards(q, k, v, links, counts):
    ranks = lax.axis_size("rank")
    across = lambda x, to: lax.ppermute(x, "rank", [(i, to(i) % ranks) for i in range(ranks)])
    core = lambda x: across(x, lambda i: i ^ 1)
    to_a = lambda x: lax.ppermute(x, "group", [(i, i ^ 1) for i in range(4)])
    to_b = lambda x: lax.ppermute(x, "group", [(i, 3 - i) for i in range(4)])

    kv, pay_a, pay_b, table = pack(links, counts, q, k, v)
    first = across(kv, lambda i: i + 2 if i % 2 else i - 2)
    from_core = core(kv)
    got_a = [to_a(x) for x in pay_a]
    got_b = [to_b(x) for x in pay_b]
    state = local(table, q, [("own", kv), ("core", from_core)])

    back_a, back_b = [None] * PARTS, [None] * PARTS
    got_a[0], got_b[0], state = lax.optimization_barrier((got_a[0], got_b[0], state))
    kv_later, got_a[0], got_b[0] = lax.optimization_barrier((kv, got_a[0], got_b[0]))
    second = across(kv_later, lambda i: i - 2 if i % 2 else i + 2)
    part_a, part_b = remote(kv, got_a[0], got_b[0], 0)
    back_a[0], back_b[0] = to_a(part_a), to_b(part_b)

    first, part_a = lax.optimization_barrier((first, part_a))
    relay = [core(first[:ROWS]), core(first[ROWS:])]
    got_a[1], got_b[1], first = lax.optimization_barrier((got_a[1], got_b[1], first))
    part_a, part_b = remote(kv, got_a[1], got_b[1], 1)
    part_a, back_a[0] = lax.optimization_barrier((part_a, back_a[0]))
    back_a[1], back_b[1] = to_a(part_a), to_b(part_b)

    state, part_a, back_a[0], back_b[0] = lax.optimization_barrier((state, part_a, back_a[0], back_b[0]))
    middle = [("first", first), ("relay", relay), ("pairs", got_a + got_b)]
    state = local(table, q, middle, state, cost=MIDDLE_COST)
    second, state = lax.optimization_barrier((second, state))
    return local(table, q, [("second", second)], state, back_b + back_a, True)


def solution(mesh):
    rows = P(("group", "rank"), None)
    return jax.shard_map(
        shards,
        mesh=mesh,
        in_specs=(rows, rows, rows, rows, P(("group", "rank"))),
        out_specs=rows,
        check_vma=False,
    )
```

```python
import functools
import math

import jax
import jax.numpy as jnp
from jax import lax
from jax.experimental import pallas as pl
from jax.experimental.pallas import tpu as pltpu
from jax.sharding import PartitionSpec as P

H = 16
HD = 128
LMAX = 8
TILE = 128
ROWS = 256
W = 2048
HALF = W // 2
NEG = -1e30
SCALE = math.log2(math.e) / math.sqrt(HD)
PARTS = 2
PH = H // 2 // PARTS
PW = PH * HD
PAYLOAD = 3 * ROWS + 16
REPLY = PW + 16
SPLIT = 4
VMEM_LIMIT = 20 * 1024 * 1024
REMOTE_COST = (400, 200)
MIDDLE_COST = 1

f32 = jnp.float32
bf16 = jnp.bfloat16


def log_multiplicity(links_ref, counts_ref, i, cand, own):
    times = jnp.int32(1 if own else 0)
    for s in range(LMAX):
        hit = (links_ref[i, s] == cand) & (s < counts_ref[i])
        times = times + hit.astype(jnp.int32)
    return jnp.where(times == 0, NEG, jnp.where(times == 1, 0.0, 1.0)).astype(f32)


def score(q, sources):
    raw, tops = [], []
    for k, _, bias in sources:
        s = lax.dot_general(k, q, (((1,), (1,)), ((), ())), preferred_element_type=f32)
        for j in range(2):
            block = s[j * TILE : (j + 1) * TILE]
            raw.append((block, bias[j]))
            tops.append(jnp.max(block, axis=0, keepdims=True) * SCALE + bias[j])
    return raw, tops


def weigh(scored, before=None, reply=None):
    raw, tops = scored
    tops = tops + [before[0] if before is not None else jnp.full_like(tops[0], 0.5 * NEG)]
    if reply is not None:
        tops = tops + [reply[1]]
    m = functools.reduce(jnp.maximum, tops)
    p = [jnp.exp2(block * SCALE + (bias - m)).astype(bf16) for block, bias in raw]
    return m, jnp.concatenate(p, axis=0)


def mix(weighed, sources, before=None, reply=None):
    m, p = weighed
    values = jnp.concatenate([v.T for _, v, _ in sources], axis=1)
    values = jnp.concatenate([values, jnp.ones((16, values.shape[1]), bf16)], axis=0)
    both = jnp.dot(values, p, preferred_element_type=f32)
    acc, l = both[:HD], both[HD : HD + 1]
    if before is not None:
        a = jnp.exp2(before[0] - m)
        acc = acc + before[2] * a
        l = l + before[1] * a
    if reply is not None:
        a = jnp.exp2(reply[1] - m)
        acc = acc + reply[0].astype(f32) * a
        l = l + a
    return m, l, acc


def over_heads(heads, load, store):
    held, scored, weighed = {}, {}, {}
    for t in range(heads + 2):
        if t < heads:
            held[t] = load(t)
            scored[t] = score(*held[t][:2])
        if 0 <= t - 1 < heads:
            weighed[t - 1] = weigh(scored.pop(t - 1), *held[t - 1][2:])
        if t >= 2:
            _, sources, before, reply = held.pop(t - 2)
            store(t - 2, *mix(weighed.pop(t - 2), sources, before, reply))


def payload_heads(way, part):
    return way * HALF + part * PW, (1 - way) * HALF + part * PW


def pack_kernel(links_hbm, counts_hbm, q_hbm, k_hbm, v_hbm, kv_ref, *refs):
    pay_refs, table_ref = refs[: 2 * PARTS], refs[2 * PARTS]
    links_ref, counts_ref, small_sems, sems = refs[2 * PARTS + 1 :]
    small = [
        pltpu.make_async_copy(links_hbm, links_ref, small_sems.at[0]),
        pltpu.make_async_copy(counts_hbm, counts_ref, small_sems.at[1]),
    ]
    for copy in small:
        copy.start()
    copies = []

    def begin(src, dst):
        copies.append(pltpu.make_async_copy(src, dst, sems.at[len(copies)]))
        copies[-1].start()

    step = ROWS // SPLIT
    for n, hbm in enumerate((k_hbm, v_hbm)):
        for i in range(SPLIT):
            begin(hbm.at[pl.ds(i * step, step)], kv_ref.at[pl.ds(n * ROWS + i * step, step)])
    for n, ref in enumerate(pay_refs):
        column = payload_heads(n // PARTS, n % PARTS)[1]
        begin(q_hbm.at[:, pl.ds(column, PW)], ref.at[pl.ds(2 * ROWS, ROWS)])
    for copy in small:
        copy.wait()
    bias = [
        [log_multiplicity(links_ref, counts_ref, i, c, c == i) for i in range(2)]
        for c in range(16)
    ]
    lane = lax.broadcasted_iota(jnp.int32, (16, ROWS), 1)
    row = lax.broadcasted_iota(jnp.int32, (16, ROWS), 0)
    table = jnp.zeros((16, ROWS), f32)
    for c in range(16):
        table = jnp.where(row == c, jnp.where(lane < TILE, bias[c][0], bias[c][1]), table)
    table_ref[...] = table
    even = (lax.axis_index("group") % 2) == 0
    row = lax.broadcasted_iota(jnp.int32, (16, 128), 0)
    for way in range(2):
        extra = jnp.zeros((16, 128), f32)
        for i in range(2):
            for j in range(2):
                one, three = bias[10 + j][i], bias[14 + j][i]
                near = jnp.where(even, one, three) if way == 0 else jnp.where(even, three, one)
                extra = jnp.where(row == 4 * i + j, near, extra)
                extra = jnp.where(row == 4 * i + 2 + j, bias[12 + j][i], extra)
        for ref in pay_refs[way * PARTS : (way + 1) * PARTS]:
            ref[3 * ROWS :, 0:128] = extra.astype(bf16)
            ref[3 * ROWS :, 128:] = jnp.zeros((16, PW - 128), bf16)
    for part in range(2 * SPLIT):
        copies[part].wait()
        rows = slice(part * step, (part + 1) * step)
        for n, ref in enumerate(pay_refs):
            column = payload_heads(n // PARTS, n % PARTS)[0]
            ref[rows] = kv_ref[rows, column : column + PW]
    for copy in copies[2 * SPLIT :]:
        copy.wait()


def pack(links, counts, q, k, v):
    vmem = pl.BlockSpec(memory_space=pltpu.VMEM)
    hbm = pl.BlockSpec(memory_space=pltpu.HBM)
    args = [pltpu.with_memory_space_constraint(x, pltpu.HBM) for x in (links, counts, q, k, v)]
    out = pl.pallas_call(
        pack_kernel,
        in_specs=[hbm] * 5,
        out_specs=[vmem] * (2 + 2 * PARTS),
        out_shape=[jax.ShapeDtypeStruct((2 * ROWS, W), bf16)]
        + [jax.ShapeDtypeStruct((PAYLOAD, PW), bf16)] * (2 * PARTS)
        + [jax.ShapeDtypeStruct((16, ROWS), f32)],
        scratch_shapes=[
            pltpu.SMEM((2, LMAX), jnp.int32),
            pltpu.SMEM((2,), jnp.int32),
            pltpu.SemaphoreType.DMA((2,)),
            pltpu.SemaphoreType.DMA((2 * SPLIT + 2 * PARTS,)),
        ],
        compiler_params=pltpu.CompilerParams(vmem_limit_bytes=VMEM_LIMIT),
        cost_estimate=pl.CostEstimate(flops=0, bytes_accessed=8 * 1024 * 1024, transcendentals=0),
        name="pack",
    )(*args)
    return out[0], out[1 : 1 + PARTS], out[1 + PARTS : 1 + 2 * PARTS], out[-1]


def remote_kernel(part, kv_ref, a_ref, b_ref, out_a, out_b):
    asked, other, outs = (a_ref, b_ref), (b_ref, a_ref), (out_a, out_b)
    bias, stats = [], []
    for way in range(2):
        extra = asked[way][3 * ROWS :, 0:128].astype(f32)
        bias.append(
            [jnp.concatenate([extra[n : n + 1], extra[4 + n : 5 + n]], axis=1) for n in range(4)]
        )
        stats.append([[], [], []])

    def load(h):
        way, inner = h // PH, h % PH
        c = slice(inner * HD, (inner + 1) * HD)
        first = payload_heads(way, part)[1] + inner * HD
        own = slice(first, first + HD)
        sources = [
            (kv_ref[0:ROWS, own], kv_ref[ROWS:, own], bias[way][0:2]),
            (other[way][0:ROWS, c], other[way][ROWS : 2 * ROWS, c], bias[way][2:4]),
        ]
        return asked[way][2 * ROWS : 3 * ROWS, c], sources, None, None

    def store(h, m, l, acc):
        way, inner = h // PH, h % PH
        l = jnp.maximum(l, 1e-30)
        outs[way][inner * HD : (inner + 1) * HD] = (acc / l).astype(bf16)
        total = m + jnp.log2(l)
        high = total.astype(bf16).astype(f32)
        rest = total - high
        middle = rest.astype(bf16).astype(f32)
        for rows, piece in zip(stats[way], (high, middle, rest - middle)):
            rows.append(piece)

    over_heads(2 * PH, load, store)
    for way in range(2):
        rows = stats[way][0] + stats[way][1] + stats[way][2]
        rows += [jnp.zeros((1, ROWS), f32)] * (16 - len(rows))
        outs[way][PW:] = jnp.concatenate(rows, axis=0).astype(bf16)


def remote(kv, a, b, part):
    vmem = pl.BlockSpec(memory_space=pltpu.VMEM)
    return pl.pallas_call(
        functools.partial(remote_kernel, part),
        in_specs=[vmem] * 3,
        out_specs=[vmem] * 2,
        out_shape=[jax.ShapeDtypeStruct((REPLY, ROWS), bf16)] * 2,
        compiler_params=pltpu.CompilerParams(vmem_limit_bytes=VMEM_LIMIT),
        cost_estimate=pl.CostEstimate(
            flops=REMOTE_COST[part] * ROWS * ROWS * HALF, bytes_accessed=1024 * 1024, transcendentals=0
        ),
        name=f"remote_{part}",
    )(kv, a, b)


def local_kernel(plan, has_before, has_reply, last, *refs):
    refs = list(refs)
    table_ref, q_ref = refs.pop(0), refs.pop(0)
    odd_core = (lax.axis_index("rank") % 2) == 1
    odd_group = (lax.axis_index("group") % 2) == 1
    sources = []
    for role in plan:
        if role == "relay":
            arrays = [refs.pop(0), refs.pop(0)]
            block = jnp.where(odd_core, 3, 2)
            blocks = (block, block)
        elif role == "pairs":
            arrays = [refs.pop(0) for _ in range(2 * PARTS)]
            blocks = (jnp.where(odd_group, 7, 5), jnp.where(odd_group, 5, 7))
        else:
            arrays = refs.pop(0)
            block = {
                "own": 0,
                "core": jnp.where(odd_core, 2, 3),
                "first": jnp.where(odd_core, 1, 4),
                "second": jnp.where(odd_core, 4, 1),
            }[role]
            blocks = (block, block)
        bias = [
            [table_ref[pl.ds(block * 2 + j, 1), :] for j in range(2)] for block in blocks
        ]
        sources.append((role, arrays, bias))
    if has_before:
        acc_in, ml_in = refs.pop(0), refs.pop(0)
    if has_reply:
        reply_refs = [refs.pop(0) for _ in range(2 * PARTS)]
        totals = []
        for ref in reply_refs:
            tail = ref[PW:].astype(f32)
            totals.append(tail[0:PH] + tail[PH : 2 * PH] + tail[2 * PH : 3 * PH])
    tops, sums, copies = [], [], []

    def load(h):
        piece, inner = h // PH, h % PH
        half = h // (H // 2)
        c = slice(h * HD, (h + 1) * HD)
        low = slice(inner * HD, (inner + 1) * HD)
        given = []
        for role, arrays, bias in sources:
            if role == "relay":
                given.append((arrays[0][:, c], arrays[1][:, c], bias[half]))
                continue
            array, at = (arrays[piece], low) if role == "pairs" else (arrays, c)
            given.append((array[0:ROWS, at], array[ROWS : 2 * ROWS, at], bias[half]))
        before = reply = None
        if has_before:
            before = (ml_in[h : h + 1], ml_in[H + h : H + h + 1], acc_in[c])
        if has_reply:
            reply = (reply_refs[piece][low], totals[piece][inner : inner + 1])
        return q_ref[:, c], given, before, reply

    def store(h, m, l, acc):
        c = slice(h * HD, (h + 1) * HD)
        if last:
            out_hbm, out_ref, sems = refs
            out_ref[:, c] = (acc / l).astype(bf16).T
            copies.append(pltpu.make_async_copy(out_ref.at[:, c], out_hbm.at[:, c], sems.at[h]))
            copies[-1].start()
        else:
            refs[0][c] = acc
            tops.append(m)
            sums.append(l)

    over_heads(H, load, store)
    for copy in copies:
        copy.wait()
    if not last:
        refs[1][...] = jnp.concatenate(tops + sums, axis=0)


def local(table, q, sources, before=None, reply=None, last=False, cost=1):
    vmem = pl.BlockSpec(memory_space=pltpu.VMEM)
    plan = tuple(role for role, _ in sources)
    args = [table, q]
    for role, arrays in sources:
        args += list(arrays) if role in ("pairs", "relay") else [arrays]
    args += list(before or ()) + list(reply or ())
    if last:
        out_specs = pl.BlockSpec(memory_space=pl.ANY)
        out_shape = jax.ShapeDtypeStruct((ROWS, W), bf16)
        scratch = [pltpu.VMEM((ROWS, W), bf16), pltpu.SemaphoreType.DMA((H,))]
    else:
        scratch = []
        out_specs = [vmem, vmem]
        out_shape = [
            jax.ShapeDtypeStruct((W, ROWS), f32),
            jax.ShapeDtypeStruct((2 * H, ROWS), f32),
        ]
    return pl.pallas_call(
        functools.partial(local_kernel, plan, before is not None, reply is not None, last),
        in_specs=[vmem] * len(args),
        out_specs=out_specs,
        out_shape=out_shape,
        scratch_shapes=scratch,
        compiler_params=pltpu.CompilerParams(vmem_limit_bytes=VMEM_LIMIT),
        cost_estimate=pl.CostEstimate(
            flops=4 * cost * ROWS * ROWS * W, bytes_accessed=1024 * 1024, transcendentals=0
        ),
        name="local_" + "_".join(plan),
    )(*args)


def shards(q, k, v, links, counts):
    ranks = lax.axis_size("rank")
    across = lambda x, to: lax.ppermute(x, "rank", [(i, to(i) % ranks) for i in range(ranks)])
    core = lambda x: across(x, lambda i: i ^ 1)
    to_a = lambda x: lax.ppermute(x, "group", [(i, i ^ 1) for i in range(4)])
    to_b = lambda x: lax.ppermute(x, "group", [(i, 3 - i) for i in range(4)])

    kv, pay_a, pay_b, table = pack(links, counts, q, k, v)
    first = across(kv, lambda i: i + 2 if i % 2 else i - 2)
    from_core = core(kv)
    got_a = [to_a(x) for x in pay_a]
    got_b = [to_b(x) for x in pay_b]
    state = local(table, q, [("own", kv), ("core", from_core)])

    back_a, back_b = [None] * PARTS, [None] * PARTS
    got_a[0], got_b[0], state = lax.optimization_barrier((got_a[0], got_b[0], state))
    kv_later, got_a[0], got_b[0] = lax.optimization_barrier((kv, got_a[0], got_b[0]))
    second = across(kv_later, lambda i: i - 2 if i % 2 else i + 2)
    part_a, part_b = remote(kv, got_a[0], got_b[0], 0)
    back_a[0], back_b[0] = to_a(part_a), to_b(part_b)

    first, part_a = lax.optimization_barrier((first, part_a))
    relay = [core(first[:ROWS]), core(first[ROWS:])]
    got_a[1], got_b[1], first = lax.optimization_barrier((got_a[1], got_b[1], first))
    part_a, part_b = remote(kv, got_a[1], got_b[1], 1)
    part_a, back_a[0] = lax.optimization_barrier((part_a, back_a[0]))
    back_a[1], back_b[1] = to_a(part_a), to_b(part_b)

    state, part_a, back_a[0], back_b[0] = lax.optimization_barrier((state, part_a, back_a[0], back_b[0]))
    middle = [("first", first), ("relay", relay), ("pairs", got_a + got_b)]
    state = local(table, q, middle, state, cost=MIDDLE_COST)
    second, state = lax.optimization_barrier((second, state))
    return local(table, q, [("second", second)], state, back_b + back_a, True)


def solution(mesh):
    rows = P(("group", "rank"), None)
    return jax.shard_map(
        shards,
        mesh=mesh,
        in_specs=(rows, rows, rows, rows, P(("group", "rank"))),
        out_specs=rows,
        check_vma=False,
    )
```

```python
import functools
import math

import jax
import jax.numpy as jnp
from jax import lax
from jax.experimental import pallas as pl
from jax.experimental.pallas import tpu as pltpu
from jax.sharding import PartitionSpec as P

H = 16
HD = 128
LMAX = 8
TILE = 128
ROWS = 256
W = 2048
HALF = W // 2
NEG = -1e30
SCALE = math.log2(math.e) / math.sqrt(HD)
PARTS = 2
PH = H // 2 // PARTS
PW = PH * HD
PAYLOAD = 3 * ROWS + 16
REPLY = PW + 16
SPLIT = 4
VMEM_LIMIT = 20 * 1024 * 1024
REMOTE_COST = (400, 200)
MIDDLE_COST = 1

f32 = jnp.float32
bf16 = jnp.bfloat16


def log_multiplicity(links_ref, counts_ref, i, cand, own):
    times = jnp.int32(1 if own else 0)
    for s in range(LMAX):
        hit = (links_ref[i, s] == cand) & (s < counts_ref[i])
        times = times + hit.astype(jnp.int32)
    return jnp.where(times == 0, NEG, jnp.where(times == 1, 0.0, 1.0)).astype(f32)


def score(q, sources):
    raw, tops = [], []
    for k, _, bias in sources:
        s = lax.dot_general(k, q, (((1,), (1,)), ((), ())), preferred_element_type=f32)
        for j in range(2):
            block = s[j * TILE : (j + 1) * TILE]
            raw.append((block, bias[j]))
            tops.append(jnp.max(block, axis=0, keepdims=True) * SCALE + bias[j])
    return raw, tops


def weigh(scored, before=None, reply=None):
    raw, tops = scored
    tops = tops + [before[0] if before is not None else jnp.full_like(tops[0], 0.5 * NEG)]
    if reply is not None:
        tops = tops + [reply[1]]
    m = functools.reduce(jnp.maximum, tops)
    p = [jnp.exp2(block * SCALE + (bias - m)).astype(bf16) for block, bias in raw]
    return m, jnp.concatenate(p, axis=0)


def mix(weighed, sources, before=None, reply=None):
    m, p = weighed
    values = jnp.concatenate([v.T for _, v, _ in sources], axis=1)
    values = jnp.concatenate([values, jnp.ones((16, values.shape[1]), bf16)], axis=0)
    both = jnp.dot(values, p, preferred_element_type=f32)
    acc, l = both[:HD], both[HD : HD + 1]
    if before is not None:
        a = jnp.exp2(before[0] - m)
        acc = acc + before[2] * a
        l = l + before[1] * a
    if reply is not None:
        a = jnp.exp2(reply[1] - m)
        acc = acc + reply[0].astype(f32) * a
        l = l + a
    return m, l, acc


def over_heads(heads, load, store):
    held, scored, weighed = {}, {}, {}
    for t in range(heads + 2):
        if t < heads:
            held[t] = load(t)
            scored[t] = score(*held[t][:2])
        if 0 <= t - 1 < heads:
            weighed[t - 1] = weigh(scored.pop(t - 1), *held[t - 1][2:])
        if t >= 2:
            _, sources, before, reply = held.pop(t - 2)
            store(t - 2, *mix(weighed.pop(t - 2), sources, before, reply))


def payload_heads(way, part):
    return way * HALF + part * PW, (1 - way) * HALF + part * PW


def pack_kernel(links_hbm, counts_hbm, q_hbm, k_hbm, v_hbm, kv_ref, *refs):
    pay_refs, table_ref = refs[: 2 * PARTS], refs[2 * PARTS]
    links_ref, counts_ref, small_sems, sems = refs[2 * PARTS + 1 :]
    small = [
        pltpu.make_async_copy(links_hbm, links_ref, small_sems.at[0]),
        pltpu.make_async_copy(counts_hbm, counts_ref, small_sems.at[1]),
    ]
    for copy in small:
        copy.start()
    copies = []

    def begin(src, dst):
        copies.append(pltpu.make_async_copy(src, dst, sems.at[len(copies)]))
        copies[-1].start()

    step = ROWS // SPLIT
    for n, hbm in enumerate((k_hbm, v_hbm)):
        for i in range(SPLIT):
            begin(hbm.at[pl.ds(i * step, step)], kv_ref.at[pl.ds(n * ROWS + i * step, step)])
    for n, ref in enumerate(pay_refs):
        column = payload_heads(n // PARTS, n % PARTS)[1]
        begin(q_hbm.at[:, pl.ds(column, PW)], ref.at[pl.ds(2 * ROWS, ROWS)])
    for copy in small:
        copy.wait()
    bias = [
        [log_multiplicity(links_ref, counts_ref, i, c, c == i) for i in range(2)]
        for c in range(16)
    ]
    lane = lax.broadcasted_iota(jnp.int32, (16, ROWS), 1)
    row = lax.broadcasted_iota(jnp.int32, (16, ROWS), 0)
    table = jnp.zeros((16, ROWS), f32)
    for c in range(16):
        table = jnp.where(row == c, jnp.where(lane < TILE, bias[c][0], bias[c][1]), table)
    table_ref[...] = table
    even = (lax.axis_index("group") % 2) == 0
    row = lax.broadcasted_iota(jnp.int32, (16, 128), 0)
    for way in range(2):
        extra = jnp.zeros((16, 128), f32)
        for i in range(2):
            for j in range(2):
                one, three = bias[10 + j][i], bias[14 + j][i]
                near = jnp.where(even, one, three) if way == 0 else jnp.where(even, three, one)
                extra = jnp.where(row == 4 * i + j, near, extra)
                extra = jnp.where(row == 4 * i + 2 + j, bias[12 + j][i], extra)
        for ref in pay_refs[way * PARTS : (way + 1) * PARTS]:
            ref[3 * ROWS :, 0:128] = extra.astype(bf16)
            ref[3 * ROWS :, 128:] = jnp.zeros((16, PW - 128), bf16)
    for part in range(2 * SPLIT):
        copies[part].wait()
        rows = slice(part * step, (part + 1) * step)
        for n, ref in enumerate(pay_refs):
            column = payload_heads(n // PARTS, n % PARTS)[0]
            ref[rows] = kv_ref[rows, column : column + PW]
    for copy in copies[2 * SPLIT :]:
        copy.wait()


def pack(links, counts, q, k, v):
    vmem = pl.BlockSpec(memory_space=pltpu.VMEM)
    hbm = pl.BlockSpec(memory_space=pltpu.HBM)
    args = [pltpu.with_memory_space_constraint(x, pltpu.HBM) for x in (links, counts, q, k, v)]
    out = pl.pallas_call(
        pack_kernel,
        in_specs=[hbm] * 5,
        out_specs=[vmem] * (2 + 2 * PARTS),
        out_shape=[jax.ShapeDtypeStruct((2 * ROWS, W), bf16)]
        + [jax.ShapeDtypeStruct((PAYLOAD, PW), bf16)] * (2 * PARTS)
        + [jax.ShapeDtypeStruct((16, ROWS), f32)],
        scratch_shapes=[
            pltpu.SMEM((2, LMAX), jnp.int32),
            pltpu.SMEM((2,), jnp.int32),
            pltpu.SemaphoreType.DMA((2,)),
            pltpu.SemaphoreType.DMA((2 * SPLIT + 2 * PARTS,)),
        ],
        compiler_params=pltpu.CompilerParams(vmem_limit_bytes=VMEM_LIMIT),
        cost_estimate=pl.CostEstimate(flops=0, bytes_accessed=8 * 1024 * 1024, transcendentals=0),
        name="pack",
    )(*args)
    return out[0], out[1 : 1 + PARTS], out[1 + PARTS : 1 + 2 * PARTS], out[-1]


def remote_kernel(part, kv_ref, a_ref, b_ref, out_a, out_b):
    asked, other, outs = (a_ref, b_ref), (b_ref, a_ref), (out_a, out_b)
    bias, stats = [], []
    for way in range(2):
        extra = asked[way][3 * ROWS :, 0:128].astype(f32)
        bias.append(
            [jnp.concatenate([extra[n : n + 1], extra[4 + n : 5 + n]], axis=1) for n in range(4)]
        )
        stats.append([[], [], []])

    def load(h):
        way, inner = h // PH, h % PH
        c = slice(inner * HD, (inner + 1) * HD)
        first = payload_heads(way, part)[1] + inner * HD
        own = slice(first, first + HD)
        sources = [
            (kv_ref[0:ROWS, own], kv_ref[ROWS:, own], bias[way][0:2]),
            (other[way][0:ROWS, c], other[way][ROWS : 2 * ROWS, c], bias[way][2:4]),
        ]
        return asked[way][2 * ROWS : 3 * ROWS, c], sources, None, None

    def store(h, m, l, acc):
        way, inner = h // PH, h % PH
        l = jnp.maximum(l, 1e-30)
        outs[way][inner * HD : (inner + 1) * HD] = (acc / l).astype(bf16)
        total = m + jnp.log2(l)
        high = total.astype(bf16).astype(f32)
        rest = total - high
        middle = rest.astype(bf16).astype(f32)
        for rows, piece in zip(stats[way], (high, middle, rest - middle)):
            rows.append(piece)

    over_heads(2 * PH, load, store)
    for way in range(2):
        rows = stats[way][0] + stats[way][1] + stats[way][2]
        rows += [jnp.zeros((1, ROWS), f32)] * (16 - len(rows))
        outs[way][PW:] = jnp.concatenate(rows, axis=0).astype(bf16)


def remote(kv, a, b, part):
    vmem = pl.BlockSpec(memory_space=pltpu.VMEM)
    return pl.pallas_call(
        functools.partial(remote_kernel, part),
        in_specs=[vmem] * 3,
        out_specs=[vmem] * 2,
        out_shape=[jax.ShapeDtypeStruct((REPLY, ROWS), bf16)] * 2,
        compiler_params=pltpu.CompilerParams(vmem_limit_bytes=VMEM_LIMIT),
        cost_estimate=pl.CostEstimate(
            flops=REMOTE_COST[part] * ROWS * ROWS * HALF, bytes_accessed=1024 * 1024, transcendentals=0
        ),
        name=f"remote_{part}",
    )(kv, a, b)


def local_kernel(plan, has_before, has_reply, last, *refs):
    refs = list(refs)
    table_ref, q_ref = refs.pop(0), refs.pop(0)
    odd_core = (lax.axis_index("rank") % 2) == 1
    odd_group = (lax.axis_index("group") % 2) == 1
    sources = []
    for role in plan:
        if role == "relay":
            arrays = [refs.pop(0), refs.pop(0)]
            block = jnp.where(odd_core, 3, 2)
            blocks = (block, block)
        elif role == "pairs":
            arrays = [refs.pop(0) for _ in range(2 * PARTS)]
            blocks = (jnp.where(odd_group, 7, 5), jnp.where(odd_group, 5, 7))
        else:
            arrays = refs.pop(0)
            block = {
                "own": 0,
                "core": jnp.where(odd_core, 2, 3),
                "first": jnp.where(odd_core, 1, 4),
                "second": jnp.where(odd_core, 4, 1),
            }[role]
            blocks = (block, block)
        bias = [
            [table_ref[pl.ds(block * 2 + j, 1), :] for j in range(2)] for block in blocks
        ]
        sources.append((role, arrays, bias))
    if has_before:
        acc_in, ml_in = refs.pop(0), refs.pop(0)
    if has_reply:
        reply_refs = [refs.pop(0) for _ in range(2 * PARTS)]
        totals = []
        for ref in reply_refs:
            tail = ref[PW:].astype(f32)
            totals.append(tail[0:PH] + tail[PH : 2 * PH] + tail[2 * PH : 3 * PH])
    tops, sums, copies = [], [], []

    def load(h):
        piece, inner = h // PH, h % PH
        half = h // (H // 2)
        c = slice(h * HD, (h + 1) * HD)
        low = slice(inner * HD, (inner + 1) * HD)
        given = []
        for role, arrays, bias in sources:
            if role == "relay":
                given.append((arrays[0][:, c], arrays[1][:, c], bias[half]))
                continue
            array, at = (arrays[piece], low) if role == "pairs" else (arrays, c)
            given.append((array[0:ROWS, at], array[ROWS : 2 * ROWS, at], bias[half]))
        before = reply = None
        if has_before:
            before = (ml_in[h : h + 1], ml_in[H + h : H + h + 1], acc_in[c])
        if has_reply:
            reply = (reply_refs[piece][low], totals[piece][inner : inner + 1])
        return q_ref[:, c], given, before, reply

    def store(h, m, l, acc):
        c = slice(h * HD, (h + 1) * HD)
        if last:
            out_hbm, out_ref, sems = refs
            out_ref[:, c] = (acc / l).astype(bf16).T
            copies.append(pltpu.make_async_copy(out_ref.at[:, c], out_hbm.at[:, c], sems.at[h]))
            copies[-1].start()
        else:
            refs[0][c] = acc
            tops.append(m)
            sums.append(l)

    over_heads(H, load, store)
    for copy in copies:
        copy.wait()
    if not last:
        refs[1][...] = jnp.concatenate(tops + sums, axis=0)


def local(table, q, sources, before=None, reply=None, last=False, cost=1):
    vmem = pl.BlockSpec(memory_space=pltpu.VMEM)
    plan = tuple(role for role, _ in sources)
    args = [table, q]
    for role, arrays in sources:
        args += list(arrays) if role in ("pairs", "relay") else [arrays]
    args += list(before or ()) + list(reply or ())
    if last:
        out_specs = pl.BlockSpec(memory_space=pl.ANY)
        out_shape = jax.ShapeDtypeStruct((ROWS, W), bf16)
        scratch = [pltpu.VMEM((ROWS, W), bf16), pltpu.SemaphoreType.DMA((H,))]
    else:
        scratch = []
        out_specs = [vmem, vmem]
        out_shape = [
            jax.ShapeDtypeStruct((W, ROWS), f32),
            jax.ShapeDtypeStruct((2 * H, ROWS), f32),
        ]
    return pl.pallas_call(
        functools.partial(local_kernel, plan, before is not None, reply is not None, last),
        in_specs=[vmem] * len(args),
        out_specs=out_specs,
        out_shape=out_shape,
        scratch_shapes=scratch,
        compiler_params=pltpu.CompilerParams(vmem_limit_bytes=VMEM_LIMIT),
        cost_estimate=pl.CostEstimate(
            flops=4 * cost * ROWS * ROWS * W, bytes_accessed=1024 * 1024, transcendentals=0
        ),
        name="local_" + "_".join(plan),
    )(*args)


def shards(q, k, v, links, counts):
    ranks = lax.axis_size("rank")
    across = lambda x, to: lax.ppermute(x, "rank", [(i, to(i) % ranks) for i in range(ranks)])
    core = lambda x: across(x, lambda i: i ^ 1)
    to_a = lambda x: lax.ppermute(x, "group", [(i, i ^ 1) for i in range(4)])
    to_b = lambda x: lax.ppermute(x, "group", [(i, 3 - i) for i in range(4)])

    kv, pay_a, pay_b, table = pack(links, counts, q, k, v)
    first = across(kv, lambda i: i + 2 if i % 2 else i - 2)
    from_core = core(kv)
    got_a = [to_a(x) for x in pay_a]
    got_b = [to_b(x) for x in pay_b]

    back_a, back_b = [None] * PARTS, [None] * PARTS
    kv_later, got_a[0], from_core = lax.optimization_barrier((kv, got_a[0], from_core))
    second = across(kv_later, lambda i: i - 2 if i % 2 else i + 2)
    state = local(table, q, [("own", kv), ("core", from_core)])
    got_b[0], state = lax.optimization_barrier((got_b[0], state))
    part_a, part_b = remote(kv, got_a[0], got_b[0], 0)
    back_a[0], back_b[0] = to_a(part_a), to_b(part_b)

    first, part_a = lax.optimization_barrier((first, part_a))
    relay = [core(first[:ROWS]), core(first[ROWS:])]
    got_a[1], got_b[1], first = lax.optimization_barrier((got_a[1], got_b[1], first))
    part_a, part_b = remote(kv, got_a[1], got_b[1], 1)
    part_a, back_a[0] = lax.optimization_barrier((part_a, back_a[0]))
    back_a[1], back_b[1] = to_a(part_a), to_b(part_b)

    state, part_a, back_a[0], back_b[0] = lax.optimization_barrier((state, part_a, back_a[0], back_b[0]))
    middle = [("first", first), ("relay", relay), ("pairs", got_a + got_b)]
    state = local(table, q, middle, state, cost=MIDDLE_COST)
    second, state = lax.optimization_barrier((second, state))
    return local(table, q, [("second", second)], state, back_b + back_a, True)


def solution(mesh):
    rows = P(("group", "rank"), None)
    return jax.shard_map(
        shards,
        mesh=mesh,
        in_specs=(rows, rows, rows, rows, P(("group", "rank"))),
        out_specs=rows,
        check_vma=False,
    )
```
